32 devices in a mesh: cols: 2 (over core), space: 16 (over z, y, x).
Axes of the slice: x: 2, y: 2, z: 4, core: 2. Of those that a mesh axis runs over, the one named last changes fastest.
Arguments:
- mean_state: float32 [6, 256, 256], P(None, 'space', 'cols'), may hold values from -2 to 2
- covariance: float32 [128, 6, 256, 256], P('cols', None, 'space'), may hold values from -2 to 2
- land_mask: int32 [256, 256], replicated, may hold values 0 or 1
- stations: int32 [2048], P('space'), may hold values from 0 to 65535, as said below
- observed: float32 [2048], P('space'), may hold values from -5 to 5
- obs_weight: float32 [2048], P('space'), may hold values from 0.5 to 4
Outputs:
- mean_analysis: float32 [6, 256, 256], P(None, 'space', 'cols')
- covariance_analysis: float32 [128, 6, 256, 256], P('cols', None, 'space')
The draws below stay inside these ranges and needn't reach their ends.
Inputs may be any that keep to these rules, and one draw needn't show every extreme that they name: Stations b * 128 to (b + 1) * 128 - 1 lie in grid rows b * 16 to (b + 1) * 16 - 1; several stations may share a cell.
All inputs are finite; a program needn't handle non-finite values.
Results may differ from the reference program's by a relative error of at most 0.0053.
Values may be sent and summed in bfloat16 or wider, within the bound.
No kernel may reach another device: no remote copies, remote signals or barrier semaphores. Data moves between devices by JAX's collectives and lax.ppermute only.
A program may use at most 128 MiB of HBM per device.

```python
import math
import jax
import jax.numpy as jnp
from jax import lax

ROWS = 16
NY = 256
K = 128
OBS_DEV = 128
ITERS = 4
NX = 256
NOBS = 2048


def draw_stations(key, part):
    blocks = NOBS // OBS_DEV
    local_cells = jax.random.randint(key, (blocks, OBS_DEV), 0, ROWS * NY)
    offset = jnp.arange(blocks, dtype=jnp.int32)[:, None] * (ROWS * NY)
    return (local_cells + offset).reshape(-1).astype(jnp.int32)


def draw_covariance(key, part):
    key_common = jax.random.fold_in(key, 11)
    key_own = jax.random.fold_in(key, 12)
    key_amp = jax.random.fold_in(key, 13)
    common = jax.random.normal(key_common, (6, NX, NY), jnp.float32)
    amplitude = jax.random.uniform(key_amp, (K, 1, 1, 1), jnp.float32, 0.4, 1.0)
    own = jax.random.normal(key_own, (K, 6, NX, NY), jnp.float32)
    values = 0.3 * (0.7 * amplitude * common[None] + 0.7 * own)
    return jnp.clip(values, -2.0, 2.0).astype(jnp.float32)


def place_ends(values, key, smallest, top_value):
    shape = values.shape
    index_at = [jax.random.randint(jax.random.fold_in(key, axis), (), 0, shape[axis]) for axis in range(len(shape))]
    values = values.at[tuple(index_at)].set(smallest)
    longest = shape.index(max(shape))
    index_at[longest] = (index_at[longest] + 1) % shape[longest]
    return values.at[tuple(index_at)].set(top_value)


def shard_levels(key, shape, split, least, top_value):
    def one(dim, blocks):
        steps = jax.random.uniform(jax.random.fold_in(jax.random.fold_in(key, 6), dim), (blocks,), jnp.float32, least / len(split), top_value / len(split))
        return jnp.repeat(jnp.exp(steps), shape[dim] // blocks).reshape((-1,) + (1,) * (len(shape) - dim - 1))

    factor_of = one(*split[0])
    for cut in split[1:]:
        factor_of = factor_of * one(*cut)
    return factor_of


def gaussian(stream_key, shape, width, reach, split=(), held_as=jnp.bfloat16):
    array = jax.random.normal(stream_key, shape, jnp.float32) * width
    if len(split) > 0:
        array = shard_levels(stream_key, shape, split, -0.22, 0.18) * array
    return jnp.clip(array, min=-reach, max=reach).astype(held_as)


def setup_inputs(seed: int = 0) -> dict:
    arg_keys = jax.random.split(jax.random.key(seed), 7)
    return {
        "mean_state": gaussian(arg_keys[0], (6, NX, NY), 0.5, 2.0, ((1, 16), (2, 2)), jnp.float32),
        "covariance": draw_covariance(jax.random.fold_in(arg_keys[6], 71), 0),
        "land_mask": place_ends((jax.random.randint(arg_keys[2], (NX, NY), 0, 10) < 9).astype(jnp.int32), jax.random.fold_in(arg_keys[2], 1), 0, 1),
        "stations": draw_stations(jax.random.fold_in(arg_keys[6], 71), 0),
        "observed": gaussian(arg_keys[4], (NOBS,), 1.0, 5.0, ((0, 16),), jnp.float32),
        "obs_weight": jnp.clip(jnp.exp(math.log(4.0) - 2.0794415 * jax.random.uniform(arg_keys[5], (NOBS,), jnp.float32) ** shard_levels(arg_keys[5], (NOBS,), ((0, 16),), -0.2, 0.2)), 0.5, 4.0),
    }


time_step = 0.5
gravity = 1.0
reduced_gravity = 0.125
coriolis = 0.3
friction = 0.05
layer_depths = (1.0, 2.0)

def diff_rows(values):
    return 0.5 * (values[..., 2:, 1:-1] - values[..., :-2, 1:-1])

def diff_cols(values):
    return 0.5 * (values[..., 1:-1, 2:] - values[..., 1:-1, :-2])

def inner(values):
    return values[..., 1:-1, 1:-1]

def velocities(field, wet_cells):
    wet_inner = inner(wet_cells)
    surface = field[..., 0, :, :] + field[..., 3, :, :]
    pressure_top = gravity * surface
    pressure_pair = (pressure_top, pressure_top - reduced_gravity * field[..., 0, :, :])
    velocity_pairs = []
    for layer_index in range(2):
        zonal = inner(field[..., 3 * layer_index + 1, :, :])
        north = inner(field[..., 3 * layer_index + 2, :, :])
        pressure = pressure_pair[layer_index]
        zonal_new = wet_inner * (zonal + time_step * (-diff_rows(pressure) + coriolis * north - friction * zonal))
        north_new = wet_inner * (north + time_step * (-diff_cols(pressure) - coriolis * zonal - friction * north))
        velocity_pairs.append((zonal_new, north_new))
    return velocity_pairs

def mean_core(padded, wet_cells):
    velocity_pairs = velocities(padded, wet_cells)
    fields = []
    carried = []
    for layer_index in range(2):
        thickness = padded[3 * layer_index]
        column_depth = layer_depths[layer_index] + inner(thickness)
        zonal_new, north_new = velocity_pairs[layer_index]
        updated = thickness[2:-2, 2:-2] - time_step * (diff_rows(column_depth * zonal_new) + diff_cols(column_depth * north_new))
        fields += [updated, zonal_new[1:-1, 1:-1], north_new[1:-1, 1:-1]]
        carried += [thickness[1:-1, 2:-2], zonal_new[:, 1:-1], north_new[:, 1:-1]]
    return (jnp.stack(fields), jnp.stack(carried))

def tangent_core(padded, carried, wet_cells):
    beside_all = jnp.pad(carried, ((0, 0), (0, 0), (1, 1)))
    velocity_pairs = velocities(padded, wet_cells)
    fields = []
    for layer_index in range(2):
        thickness = padded[..., 3 * layer_index, :, :]
        column_depth = layer_depths[layer_index] + beside_all[3 * layer_index]
        zonal_new, north_new = velocity_pairs[layer_index]
        flux_rows = column_depth * zonal_new + inner(thickness) * beside_all[3 * layer_index + 1]
        flux_cols = column_depth * north_new + inner(thickness) * beside_all[3 * layer_index + 2]
        updated = thickness[..., 2:-2, 2:-2] - time_step * (diff_rows(flux_rows) + diff_cols(flux_cols))
        fields += [updated, zonal_new[..., 1:-1, 1:-1], north_new[..., 1:-1, 1:-1]]
    return jnp.stack(fields, axis=-3)

def reference(mean_state, covariance, land_mask, stations, observed, obs_weight):
    wet_all = jnp.pad(land_mask.astype(jnp.float32), 2)
    mean_now = mean_state
    columns = covariance
    for step_index in range(ITERS):
        mean_next, carried = mean_core(jnp.pad(mean_now, ((0, 0), (2, 2), (2, 2))), wet_all)

        def advance(column_block):
            return tangent_core(jnp.pad(column_block, ((0, 0), (0, 0), (2, 2), (2, 2))), carried, wet_all)
        blocks = columns.reshape((8, K // 8) + columns.shape[1:])
        columns = lax.map(advance, blocks).reshape(columns.shape)
        mean_now = mean_next
    surface = (mean_now[0] + mean_now[3]).reshape(-1)
    innovation = obs_weight * (observed - surface[stations])
    column_surface = (columns[:, 0] + columns[:, 3]).reshape(K, -1)
    sensed = column_surface[:, stations] * obs_weight[None, :]
    identity = jnp.eye(K, dtype=jnp.float32)
    gram_matrix = identity + jnp.dot(sensed.astype(jnp.float32), sensed.T.astype(jnp.float32), precision=lax.Precision.HIGHEST, preferred_element_type=jnp.float32)
    target = jnp.dot(sensed.astype(jnp.float32), innovation.astype(jnp.float32), precision=lax.Precision.HIGHEST, preferred_element_type=jnp.float32)
    lower_factor = lax.linalg.cholesky(gram_matrix)
    halfway = lax.linalg.triangular_solve(lower_factor, target[:, None], left_side=True, lower=True)
    weights = lax.linalg.triangular_solve(lower_factor, halfway, left_side=True, lower=True, transpose_a=True)[:, 0]
    inverse = lax.linalg.triangular_solve(lower_factor, identity, left_side=True, lower=True)
    transform = inverse.T
    increment = jnp.einsum('k,kfxy->fxy', weights, columns, precision=lax.Precision.HIGHEST)
    mean_analysis = mean_now + increment
    transform_low = transform.astype(jnp.bfloat16)
    columns_low = columns.astype(jnp.bfloat16).reshape(K, -1)
    updated = jnp.dot(transform_low.T.astype(jnp.float32), columns_low.astype(jnp.float32), preferred_element_type=jnp.float32)
    return (mean_analysis, updated.reshape(columns.shape))
```

```python
import functools

import jax
import jax.numpy as jnp
from jax import lax
from jax.experimental import pallas as pl
from jax.experimental.pallas import tpu as pltpu
from jax.sharding import PartitionSpec as P

ITERS = 4
DEPTH = 2 * ITERS
GROUP = 16

time_step = 0.5
gravity = 1.0
reduced_gravity = 0.125
coriolis = 0.3
friction = 0.05
layer_depths = (1.0, 2.0)

keep_part = 1.0 - time_step * friction
turn_part = time_step * coriolis
slope_part = 0.5 * time_step

f32 = jnp.float32
bf16 = jnp.bfloat16


def halo_rows():
    rows = []
    for layer in range(2):
        rows += [(3 * layer, d) for d in range(DEPTH, 0, -1)]
    for layer in range(2):
        rows += [(3 * layer + 1, d) for d in range(DEPTH - 1, 0, -1)]
        rows += [(3 * layer + 2, d) for d in range(DEPTH - 2, 0, -1)]
    return rows


def pack_kernel(*refs, tile_rows):
    cov_refs, up_ref, down_ref = refs[:-2], refs[-2], refs[-1]
    stride = 6 * tile_rows

    def row(field, r):
        return jnp.concatenate(
            [ref[pl.ds(field * tile_rows + r, GROUP, stride=stride), :] for ref in cov_refs],
            axis=1,
        )

    for i, (field, d) in enumerate(halo_rows()):
        for ref, r in ((up_ref, tile_rows - d), (down_ref, d - 1)):
            value = row(field, r)
            if d == DEPTH - 1 and field % 3 == 1:
                value = value + (turn_part / keep_part) * row(field + 1, r)
            ref[i] = value.astype(bf16)


def lane_steps(parts, lane):
    n = len(parts)
    right = [pltpu.roll(p, 1, 1) for p in parts]
    left = [pltpu.roll(p, 127, 1) for p in parts]
    out = []
    for i in range(n):
        before = jnp.where(lane == 0, right[i - 1] if i > 0 else 0.0, right[i])
        after = jnp.where(lane == 127, left[i + 1] if i < n - 1 else 0.0, left[i])
        out.append(after - before)
    return out


def station_hits(stations_ref, r, cells):
    position = lax.broadcasted_iota(jnp.int32, (cells, stations_ref.shape[1]), 0) + r * cells
    return position == stations_ref[...]


def mean_kernel(
    where_ref, mean_ref, mask_ref, stations_ref, observed_ref, weight_ref,
    wet_out, coef_out, final_out, innov_out, *, tile_rows, grid_rows,
):
    first_row = where_ref[0]
    ext, cells = mean_ref.shape[1:]
    wets = []
    for i in range(ext // 8):
        g = first_row - DEPTH + 8 * i
        inside = jnp.logical_and(g >= 0, g < grid_rows).astype(f32)
        start = pl.multiple_of(jnp.clip(g, 0, grid_rows - 8), 8)
        wets.append(mask_ref[pl.ds(start, 8), :].astype(f32) * inside)
    wet = jnp.concatenate(wets, axis=0)
    g_all = first_row - DEPTH + lax.broadcasted_iota(jnp.int32, (ext, cells), 0)
    keep = jnp.logical_and(g_all >= 0, g_all < grid_rows).astype(f32)
    lane_all = lax.broadcasted_iota(jnp.int32, (ext, cells), 1)

    def put(ref, index, value):
        rows = ref.shape[0] // (cells // 128)
        for c in range(cells // 128):
            ref[pl.ds(c * rows + index * ext, ext), :] = value[:, 128 * c : 128 * c + 128]

    put(wet_out, 0, wet * keep_part)
    put(wet_out, 1, wet * turn_part)
    put(wet_out, 2, wet * slope_part)

    def diff_rows(a):
        return 0.5 * (pltpu.roll(a, ext - 1, 0) - pltpu.roll(a, 1, 0))

    def diff_cols(a):
        after = jnp.where(lane_all == cells - 1, 0.0, pltpu.roll(a, cells - 1, 1))
        before = jnp.where(lane_all == 0, 0.0, pltpu.roll(a, 1, 1))
        return 0.5 * (after - before)

    state = [mean_ref[f] for f in range(6)]
    for t in range(ITERS):
        pressure_top = gravity * (state[0] + state[3])
        pressures = (pressure_top, pressure_top - reduced_gravity * state[0])
        fresh = []
        for layer in range(2):
            h, u, v = state[3 * layer : 3 * layer + 3]
            p = pressures[layer]
            u_new = wet * (u + time_step * (-diff_rows(p) + coriolis * v - friction * u))
            v_new = wet * (v + time_step * (-diff_cols(p) - coriolis * u - friction * v))
            depth = layer_depths[layer] + h
            h_new = h - time_step * (diff_rows(depth * u_new) + diff_cols(depth * v_new))
            for q, value in enumerate((depth, u_new, v_new)):
                put(coef_out, t * 6 + 3 * layer + q, slope_part * value)
            fresh += [h_new * keep, u_new, v_new]
        state = fresh
    for f in range(6):
        final_out[f] = state[f][DEPTH : DEPTH + tile_rows, :]
    surface = (state[0] + state[3])[DEPTH : DEPTH + tile_rows, :]
    n_stations = stations_ref.shape[1]
    sublane = lax.broadcasted_iota(jnp.int32, (8, n_stations), 0)
    picked = jnp.zeros((8, n_stations), f32)
    for r in range(tile_rows):
        hits = station_hits(stations_ref, r, cells).astype(f32)
        block = surface[r // 8 * 8 : r // 8 * 8 + 8, :]
        values = jnp.dot(block, hits, precision=lax.Precision.HIGHEST, preferred_element_type=f32)
        picked = picked + jnp.where(sublane == r % 8, values, 0.0)
    at_station = jnp.sum(picked, axis=0, keepdims=True)
    innovation = weight_ref[...] * (observed_ref[...] - at_station)
    innov_out[...] = jnp.where(sublane == 0, innovation, 0.0)


def window_kernel(
    where_ref, low_ref, high_ref, wet_ref, coef_ref, stations_ref, *refs,
    tile_rows, grid_rows,
):
    cov_refs, (pf_out, sensed_out, st) = refs[:-3], refs[-3:]
    first_row = where_ref[0]
    ext = tile_rows + 2 * DEPTH
    groups = len(cov_refs)
    cells = 128 * groups
    stride = 6 * tile_rows

    def fill(r, carry):
        for f in range(6):
            for c in range(groups):
                st[f, DEPTH + r, :, pl.ds(128 * c, 128)] = cov_refs[c][
                    pl.ds(f * tile_rows + r, GROUP, stride=stride), :
                ]
        return carry

    lax.fori_loop(0, tile_rows, fill, 0)
    for i, (field, d) in enumerate(halo_rows()):
        st[field, DEPTH - d] = low_ref[i].astype(f32)
        st[field, DEPTH + tile_rows + d - 1] = high_ref[i].astype(f32)
    for layer in range(2):
        for r in (1, ext - 2):
            st[3 * layer + 2, r] = jnp.zeros((GROUP, cells), f32)
    lane = lax.broadcasted_iota(jnp.int32, (8, 128), 1)

    for t in range(ITERS):
        shrink = 2 * t
        for kg in range(GROUP // 8):

            def load(field, r, kg=kg):
                return [
                    st[field, r, pl.ds(8 * kg, 8), pl.ds(128 * c, 128)] for c in range(groups)
                ]

            def store(field, r, parts, kg=kg):
                for c in range(groups):
                    st[field, r, pl.ds(8 * kg, 8), pl.ds(128 * c, 128)] = parts[c]

            def spread(ref, index, r):
                rows = ref.shape[0] // groups
                return [
                    ref[pl.ds(c * rows + index * ext + r, 8, stride=0), :] for c in range(groups)
                ]

            def pressures(h):
                top = [a + b for a, b in zip(h[0], h[1])]
                return [top, [p - reduced_gravity * a for p, a in zip(top, h[0])]]

            def body(r, carry, t=t, load=load, store=store):
                p_prev, p_here, h_here, flux_2, flux_1, part_1 = carry
                h_next = [load(0, r + 1), load(3, r + 1)]
                p_next = pressures(h_next)
                wet_a, wet_b, wet_c = (spread(wet_ref, q, r) for q in range(3))
                g = first_row - DEPTH + r - 1
                keep = jnp.where(jnp.logical_and(g >= 0, g < grid_rows), 1.0, 0.0).astype(f32)
                flux_0, part_0 = [], []
                for layer in range(2):
                    u, v = load(3 * layer + 1, r), load(3 * layer + 2, r)
                    depth, mu, mv = (
                        spread(coef_ref, t * 6 + 3 * layer + q, r) for q in range(3)
                    )
                    slope = lane_steps(p_here[layer], lane)
                    u_new, v_new, flux, cross = [], [], [], []
                    for c in range(groups):
                        u_c = (
                            wet_a[c] * u[c]
                            + wet_b[c] * v[c]
                            - wet_c[c] * (p_next[layer][c] - p_prev[layer][c])
                        )
                        v_c = wet_a[c] * v[c] - wet_b[c] * u[c] - wet_c[c] * slope[c]
                        h = h_here[layer][c]
                        u_new.append(u_c)
                        v_new.append(v_c)
                        flux.append(depth[c] * u_c + h * mu[c])
                        cross.append(depth[c] * v_c + h * mv[c])
                    store(3 * layer + 1, r, u_new)
                    store(3 * layer + 2, r, v_new)
                    cross = lane_steps(cross, lane)
                    part_0.append([h_here[layer][c] - cross[c] for c in range(groups)])
                    flux_0.append(flux)
                    store(
                        3 * layer,
                        r - 1,
                        [
                            keep * (part_1[layer][c] - (flux[c] - flux_2[layer][c]))
                            for c in range(groups)
                        ],
                    )
                return (p_here, p_next, h_next, flux_1, flux_0, part_0)

            h_a = [load(0, shrink), load(3, shrink)]
            h_b = [load(0, shrink + 1), load(3, shrink + 1)]
            nothing = [[a - a for a in h] for h in h_a]
            lax.fori_loop(
                shrink + 1,
                ext - shrink - 1,
                body,
                (pressures(h_a), pressures(h_b), h_b, nothing, nothing, nothing),
                unroll=2,
            )

    n_stations = stations_ref.shape[1]
    total = jnp.zeros((3 * GROUP, n_stations), f32)
    for r in range(tile_rows):
        for f in range(6):
            pf_out[f, r] = st[f, DEPTH + r].astype(bf16)
        surface = st[0, DEPTH + r] + st[3, DEPTH + r]
        high = surface.astype(bf16)
        rest = surface - high.astype(f32)
        middle = rest.astype(bf16)
        low = (rest - middle.astype(f32)).astype(bf16)
        pieces = jnp.concatenate([high, middle, low], axis=0)
        hits = station_hits(stations_ref, r, cells).astype(f32).astype(bf16)
        total = total + jnp.dot(pieces, hits, preferred_element_type=f32)
    sensed_out[...] = (
        total[:GROUP] + (total[GROUP : 2 * GROUP] + total[2 * GROUP : 3 * GROUP])
    )


def gram_kernel(where_ref, weight_ref, innov_ref, *refs, columns):
    sensed_refs, out_ref, both = refs[:-2], refs[-2], refs[-1]
    index = where_ref[1]
    count = len(sensed_refs)
    for d in range(count):
        start = pl.multiple_of(lax.rem(index + d, count) * columns, 8)
        both[pl.ds(start, columns), :] = sensed_refs[d][...] * weight_ref[...]
    total = count * columns
    both[pl.ds(total, 8), :] = innov_ref[...]
    out_ref[...] = lax.dot_general(
        both[...],
        both[pl.ds(0, total), :],
        (((1,), (1,)), ((), ())),
        precision=lax.Precision.HIGHEST,
        preferred_element_type=f32,
    )


def factor_kernel(where_ref, gram_ref, mix_out, scr, *, columns):
    index = where_ref[1]
    total = gram_ref.shape[1]
    blocks = total // 8
    lane = lax.broadcasted_iota(jnp.int32, (8, total), 1)
    sub = lax.broadcasted_iota(jnp.int32, (8, total), 0)
    eye = [(lane == sub + 8 * b).astype(f32) for b in range(blocks)]
    m = [gram_ref[pl.ds(8 * b, 8), :] + eye[b] for b in range(blocks)]
    w = list(eye)
    pivots = [jnp.ones((8, total), f32) for _ in range(blocks)]
    for j in range(total):
        b, i = j // 8, j % 8
        heads = {q: jnp.broadcast_to(m[q][:, j : j + 1], (8, total)) for q in range(b, blocks)}
        pivot = jnp.broadcast_to(heads[b][i : i + 1, :], (8, total))
        pivots[b] = jnp.where(sub == i, pivot, pivots[b])
        inverse = 1.0 / pivot
        row_m = jnp.broadcast_to(m[b][i : i + 1, :], (8, total)) * inverse
        row_w = jnp.broadcast_to(w[b][i : i + 1, :], (8, total)) * inverse
        for q in range(b, blocks):
            head = jnp.where(sub > i, heads[q], 0.0) if q == b else heads[q]
            m[q] = m[q] - head * row_m
            w[q] = w[q] - head * row_w
    target = gram_ref[pl.ds(total, 1), :]
    weights = jnp.zeros((1, total), f32)
    for b in range(blocks):
        inv = w[b] / jnp.sqrt(pivots[b])
        scr[pl.ds(8 * b, 8), :] = inv
        half = jnp.sum(inv * target, axis=1, keepdims=True)
        weights = weights + jnp.sum(inv * half, axis=0, keepdims=True)
    shift = lax.rem(total - index * columns, total)
    mine = scr[pl.ds(pl.multiple_of(index * columns, 8), columns), :]
    mix_out[pl.ds(0, columns), :] = pltpu.roll(mine, shift, 1).astype(bf16)
    weights = pltpu.roll(jnp.broadcast_to(weights, (8, total)), shift, 1)
    high = weights.astype(bf16)
    low = (weights - high.astype(f32)).astype(bf16)
    pad = jnp.zeros((8, total), f32)
    rows = jnp.where(sub == 0, high.astype(f32), jnp.where(sub == 1, low.astype(f32), 0.0))
    mix_out[pl.ds(columns, 16), :] = jnp.concatenate([rows, pad], axis=0).astype(bf16)


def mix_kernel(where_ref, mix_ref, mean_ref, *refs, columns):
    piece_refs, cov_out, mean_out, scr = refs[:-3], refs[-3], refs[-2], refs[-1]
    tile_rows, cells = mean_ref.shape[1:]
    piece = mean_out.shape[2]
    group = pl.program_id(1)
    mix = mix_ref[...]
    for r in range(tile_rows):
        stack = jnp.concatenate([ref[0, r] for ref in piece_refs], axis=0)
        result = jnp.dot(mix, stack, preferred_element_type=f32)
        cov_out[:, 0, r, :] = result[:columns]
        scr[group, pl.ds(r, 1), :] = (
            result[columns : columns + 1] + result[columns + 1 : columns + 2]
        )

    @pl.when(group == pl.num_programs(1) - 1)
    def _():
        change = jnp.concatenate([scr[c] for c in range(cells // 128)], axis=1)
        whole = mean_ref[0] + change
        shift = lax.rem(cells - where_ref[1] * piece, cells)
        mean_out[0] = pltpu.roll(whole, shift, 1)[:, :piece]


def spread_sum(value, axis):
    count = lax.axis_size(axis)
    if count & (count - 1):
        return lax.psum(value, axis)
    step = 1
    while step < count:
        value = value + lax.ppermute(value, axis, [(i, i ^ step) for i in range(count)])
        step *= 2
    return value


def shifted(value, axis):
    count = lax.axis_size(axis)
    return [value] + [
        lax.ppermute(value, axis, [((i + d) % count, i) for i in range(count)])
        for d in range(1, count)
    ]


def whole_spec(shape):
    return pl.BlockSpec(shape, lambda *_: (0,) * len(shape))


def local(mean_state, covariance, land_mask, stations, observed, obs_weight):
    columns, _, tile_rows, cells = covariance.shape
    piece = mean_state.shape[2]
    n_space = lax.axis_size("space")
    n_cols = lax.axis_size("cols")
    total = columns * n_cols
    grid_rows = tile_rows * n_space
    ext = tile_rows + 2 * DEPTH
    n_stations = stations.shape[0]
    chunks = columns // GROUP
    n_halo = len(halo_rows())
    groups = cells // 128
    space_index = lax.axis_index("space")
    column_index = lax.axis_index("cols")
    first_row = space_index * tile_rows
    where = jnp.stack([first_row, column_index]).astype(jnp.int32)
    up = [(i, i + 1) for i in range(n_space - 1)]
    down = [(i + 1, i) for i in range(n_space - 1)]
    smem = pl.BlockSpec(memory_space=pltpu.SMEM)

    mean_low = lax.ppermute(mean_state[:, tile_rows - DEPTH :, :], "space", up)
    mean_high = lax.ppermute(mean_state[:, :DEPTH, :], "space", down)
    mean_ext = jnp.concatenate([mean_low, mean_state, mean_high], axis=1)
    mean_ext = lax.all_gather(mean_ext, "cols", axis=2, tiled=True)

    flat = covariance.reshape(columns * 6 * tile_rows, cells)
    span = GROUP * 6 * tile_rows


    def cov_specs(c):
        return [pl.BlockSpec((span, 128), lambda i, g=g: (c, g)) for g in range(groups)]

    lows, highs = [], []
    for c in range(chunks):
        halo_shape = jax.ShapeDtypeStruct((n_halo, GROUP, cells), bf16)
        going_up, going_down = pl.pallas_call(
            functools.partial(pack_kernel, tile_rows=tile_rows),
            grid=(1,),
            in_specs=cov_specs(c),
            out_specs=[whole_spec((n_halo, GROUP, cells))] * 2,
            out_shape=[halo_shape, halo_shape],
            name=f"pack_{c}",
        )(*[flat] * groups)
        lows.append(lax.ppermute(going_up, "space", up))
        highs.append(lax.ppermute(going_down, "space", down))

    station_row = (stations - first_row * cells).astype(jnp.int32)[None, :]
    weight_row = obs_weight[None, :]
    wet, coef, mean_final, innovation = pl.pallas_call(
        functools.partial(mean_kernel, tile_rows=tile_rows, grid_rows=grid_rows),
        in_specs=[smem] + [pl.BlockSpec(memory_space=pltpu.VMEM)] * 5,
        out_specs=[pl.BlockSpec(memory_space=pltpu.VMEM)] * 4,
        out_shape=[
            jax.ShapeDtypeStruct((groups * 3 * ext, 128), f32),
            jax.ShapeDtypeStruct((groups * ITERS * 6 * ext, 128), f32),
            jax.ShapeDtypeStruct((6, tile_rows, cells), f32),
            jax.ShapeDtypeStruct((8, n_stations), f32),
        ],
        name="mean_window",
    )(where, mean_ext, land_mask, station_row, observed[None, :], weight_row)

    forecasts, sensed = [], []
    for c in range(chunks):
        pf, s = pl.pallas_call(
            functools.partial(window_kernel, tile_rows=tile_rows, grid_rows=grid_rows),
            grid=(1,),
            in_specs=[
                smem,
                whole_spec((n_halo, GROUP, cells)),
                whole_spec((n_halo, GROUP, cells)),
                whole_spec((groups * 3 * ext, 128)),
                whole_spec((groups * ITERS * 6 * ext, 128)),
                whole_spec((1, n_stations)),
            ]
            + cov_specs(c),
            out_specs=[
                whole_spec((6, tile_rows, GROUP, cells)),
                whole_spec((GROUP, n_stations)),
            ],
            out_shape=[
                jax.ShapeDtypeStruct((6, tile_rows, GROUP, cells), bf16),
                jax.ShapeDtypeStruct((GROUP, n_stations), f32),
            ],
            scratch_shapes=[pltpu.VMEM((6, ext, GROUP, cells), f32)],
            name=f"window_{c}",
        )(where, lows[c], highs[c], wet, coef, station_row, *[flat] * groups)
        forecasts.append(shifted(pf, "cols"))
        sensed.append(s)

    sensed_all = shifted(jnp.concatenate(sensed, axis=0), "cols")
    gram = pl.pallas_call(
        functools.partial(gram_kernel, columns=columns),
        in_specs=[smem] + [pl.BlockSpec(memory_space=pltpu.VMEM)] * (2 + n_cols),
        out_specs=pl.BlockSpec(memory_space=pltpu.VMEM),
        out_shape=jax.ShapeDtypeStruct((total + 8, total), f32),
        scratch_shapes=[pltpu.VMEM((total + 8, n_stations), f32)],
        name="gram",
    )(where, weight_row, innovation, *sensed_all)
    gram = spread_sum(gram, "space")
    mix = pl.pallas_call(
        functools.partial(factor_kernel, columns=columns),
        in_specs=[smem, pl.BlockSpec(memory_space=pltpu.VMEM)],
        out_specs=pl.BlockSpec(memory_space=pltpu.VMEM),
        out_shape=jax.ShapeDtypeStruct((columns + 16, total), bf16),
        scratch_shapes=[pltpu.VMEM((total, total), f32)],
        name="factor",
    )(where, gram)

    pieces = [forecasts[c][d] for d in range(n_cols) for c in range(chunks)]
    field_spec = pl.BlockSpec((1, tile_rows, GROUP, 128), lambda f, g: (f, 0, 0, g))
    updated, mean_out = pl.pallas_call(
        functools.partial(mix_kernel, columns=columns),
        grid=(6, groups),
        in_specs=[
            smem,
            whole_spec((columns + 16, total)),
            pl.BlockSpec((1, tile_rows, cells), lambda f, g: (f, 0, 0)),
        ]
        + [field_spec] * len(pieces),
        out_specs=[
            pl.BlockSpec((columns, 1, tile_rows, 128), lambda f, g: (0, f, 0, g)),
            pl.BlockSpec((1, tile_rows, piece), lambda f, g: (f, 0, 0)),
        ],
        out_shape=[
            jax.ShapeDtypeStruct((columns, 6, tile_rows, cells), f32),
            jax.ShapeDtypeStruct((6, tile_rows, piece), f32),
        ],
        scratch_shapes=[pltpu.VMEM((groups, tile_rows, 128), f32)],
        name="mix",
    )(where, mix, mean_final, *pieces)
    return (mean_out, updated)


def solution(mesh):
    return jax.shard_map(
        local,
        mesh=mesh,
        in_specs=(
            P(None, "space", "cols"),
            P("cols", None, "space", None),
            P(),
            P("space"),
            P("space"),
            P("space"),
        ),
        out_specs=(P(None, "space", "cols"), P("cols", None, "space", None)),
        check_vma=False,
    )
```

```python
import functools

import jax
import jax.numpy as jnp
from jax import lax
from jax.experimental import pallas as pl
from jax.experimental.pallas import tpu as pltpu
from jax.sharding import PartitionSpec as P

ITERS = 4
DEPTH = 2 * ITERS
GROUP = 16

time_step = 0.5
gravity = 1.0
reduced_gravity = 0.125
coriolis = 0.3
friction = 0.05
layer_depths = (1.0, 2.0)

keep_part = 1.0 - time_step * friction
turn_part = time_step * coriolis
slope_part = 0.5 * time_step

f32 = jnp.float32
bf16 = jnp.bfloat16


def halo_rows():
    rows = []
    for layer in range(2):
        rows += [(3 * layer, d) for d in range(DEPTH, 0, -1)]
    for layer in range(2):
        rows += [(3 * layer + 1, d) for d in range(DEPTH - 1, 0, -1)]
        rows += [(3 * layer + 2, d) for d in range(DEPTH - 2, 0, -1)]
    return rows


def pack_kernel(*refs, tile_rows):
    cov_refs, up_ref, down_ref = refs[:-2], refs[-2], refs[-1]
    stride = 6 * tile_rows

    def row(field, r):
        return jnp.concatenate(
            [ref[pl.ds(field * tile_rows + r, GROUP, stride=stride), :] for ref in cov_refs],
            axis=1,
        )

    for i, (field, d) in enumerate(halo_rows()):
        for ref, r in ((up_ref, tile_rows - d), (down_ref, d - 1)):
            value = row(field, r)
            if d == DEPTH - 1 and field % 3 == 1:
                value = value + (turn_part / keep_part) * row(field + 1, r)
            ref[i] = value.astype(bf16)


def lane_steps(parts, lane):
    n = len(parts)
    right = [pltpu.roll(p, 1, 1) for p in parts]
    left = [pltpu.roll(p, 127, 1) for p in parts]
    out = []
    for i in range(n):
        before = jnp.where(lane == 0, right[i - 1] if i > 0 else 0.0, right[i])
        after = jnp.where(lane == 127, left[i + 1] if i < n - 1 else 0.0, left[i])
        out.append(after - before)
    return out


def station_hits(stations_ref, r, cells):
    position = lax.broadcasted_iota(jnp.int32, (cells, stations_ref.shape[1]), 0) + r * cells
    return position == stations_ref[...]


def mean_kernel(
    where_ref, mean_ref, mask_ref, stations_ref, observed_ref, weight_ref,
    wet_out, coef_out, final_out, innov_out, *, tile_rows, grid_rows,
):
    first_row = where_ref[0]
    ext, cells = mean_ref.shape[1:]
    wets = []
    for i in range(ext // 8):
        g = first_row - DEPTH + 8 * i
        inside = jnp.logical_and(g >= 0, g < grid_rows).astype(f32)
        start = pl.multiple_of(jnp.clip(g, 0, grid_rows - 8), 8)
        wets.append(mask_ref[pl.ds(start, 8), :].astype(f32) * inside)
    wet = jnp.concatenate(wets, axis=0)
    g_all = first_row - DEPTH + lax.broadcasted_iota(jnp.int32, (ext, cells), 0)
    keep = jnp.logical_and(g_all >= 0, g_all < grid_rows).astype(f32)
    lane_all = lax.broadcasted_iota(jnp.int32, (ext, cells), 1)

    def put(ref, index, value):
        rows = ref.shape[0] // (cells // 128)
        for c in range(cells // 128):
            ref[pl.ds(c * rows + index * ext, ext), :] = value[:, 128 * c : 128 * c + 128]

    put(wet_out, 0, wet * keep_part)
    put(wet_out, 1, wet * turn_part)
    put(wet_out, 2, wet * slope_part)

    def diff_rows(a):
        return 0.5 * (pltpu.roll(a, ext - 1, 0) - pltpu.roll(a, 1, 0))

    def diff_cols(a):
        after = jnp.where(lane_all == cells - 1, 0.0, pltpu.roll(a, cells - 1, 1))
        before = jnp.where(lane_all == 0, 0.0, pltpu.roll(a, 1, 1))
        return 0.5 * (after - before)

    state = [mean_ref[f] for f in range(6)]
    for t in range(ITERS):
        pressure_top = gravity * (state[0] + state[3])
        pressures = (pressure_top, pressure_top - reduced_gravity * state[0])
        fresh = []
        for layer in range(2):
            h, u, v = state[3 * layer : 3 * layer + 3]
            p = pressures[layer]
            u_new = wet * (u + time_step * (-diff_rows(p) + coriolis * v - friction * u))
            v_new = wet * (v + time_step * (-diff_cols(p) - coriolis * u - friction * v))
            depth = layer_depths[layer] + h
            h_new = h - time_step * (diff_rows(depth * u_new) + diff_cols(depth * v_new))
            for q, value in enumerate((depth, u_new, v_new)):
                put(coef_out, t * 6 + 3 * layer + q, slope_part * value)
            fresh += [h_new * keep, u_new, v_new]
        state = fresh
    for f in range(6):
        final_out[f] = state[f][DEPTH : DEPTH + tile_rows, :]
    surface = (state[0] + state[3])[DEPTH : DEPTH + tile_rows, :]
    n_stations = stations_ref.shape[1]
    sublane = lax.broadcasted_iota(jnp.int32, (8, n_stations), 0)
    picked = jnp.zeros((8, n_stations), f32)
    for r in range(tile_rows):
        hits = station_hits(stations_ref, r, cells).astype(f32)
        block = surface[r // 8 * 8 : r // 8 * 8 + 8, :]
        values = jnp.dot(block, hits, precision=lax.Precision.HIGHEST, preferred_element_type=f32)
        picked = picked + jnp.where(sublane == r % 8, values, 0.0)
    at_station = jnp.sum(picked, axis=0, keepdims=True)
    innovation = weight_ref[...] * (observed_ref[...] - at_station)
    innov_out[...] = jnp.where(sublane == 0, innovation, 0.0)


def window_kernel(
    where_ref, low_ref, high_ref, wet_ref, coef_ref, stations_ref, *refs,
    tile_rows, grid_rows,
):
    cov_refs, (pf_out, sensed_out, state_a, state_b, press, flux) = refs[:-6], refs[-6:]
    first_row = where_ref[0]
    ext = tile_rows + 2 * DEPTH
    groups = len(cov_refs)
    cells = 128 * groups
    stride = 6 * tile_rows
    halves = range(GROUP // 8)

    def at(ref, field, r, kg):
        return [ref[field, r, pl.ds(8 * kg, 8), pl.ds(128 * c, 128)] for c in range(groups)]

    def put(ref, field, r, kg, parts):
        for c in range(groups):
            ref[field, r, pl.ds(8 * kg, 8), pl.ds(128 * c, 128)] = parts[c]

    def spread(ref, index, r):
        rows = ref.shape[0] // groups
        return [ref[pl.ds(c * rows + index * ext + r, 8, stride=0), :] for c in range(groups)]

    def fill(r, carry):
        for f in range(6):
            for c in range(groups):
                state_a[f, DEPTH + r, :, pl.ds(128 * c, 128)] = cov_refs[c][
                    pl.ds(f * tile_rows + r, GROUP, stride=stride), :
                ]
        return carry

    lax.fori_loop(0, tile_rows, fill, 0)
    for i, (field, d) in enumerate(halo_rows()):
        state_a[field, DEPTH - d] = low_ref[i].astype(f32)
        state_a[field, DEPTH + tile_rows + d - 1] = high_ref[i].astype(f32)
    for layer in range(2):
        for r in (1, ext - 2):
            state_a[3 * layer + 2, r] = jnp.zeros((GROUP, cells), f32)

    def press_of(top, bottom):
        p_top = gravity * (top + bottom)
        return p_top, p_top - reduced_gravity * top

    def first_press(r, carry):
        press[0, r], press[1, r] = press_of(state_a[0, r], state_a[3, r])
        return carry

    lax.fori_loop(0, ext, first_press, 0, unroll=2)
    lane = lax.broadcasted_iota(jnp.int32, (8, 128), 1)

    def move(t, src, dst, r_first, count):
        stores = []
        for r in [r_first + k for k in range(count)]:
            wet_a, wet_b, wet_c = (spread(wet_ref, q, r) for q in range(3))
            for layer in range(2):
                depth, mu, mv = (spread(coef_ref, t * 6 + 3 * layer + q, r) for q in range(3))
                for kg in halves:
                    h = at(src, 3 * layer, r, kg)
                    u = at(src, 3 * layer + 1, r, kg)
                    v = at(src, 3 * layer + 2, r, kg)
                    before = at(press, layer, r - 1, kg)
                    after = at(press, layer, r + 1, kg)
                    slope = lane_steps(at(press, layer, r, kg), lane)
                    u_new, v_new, along, cross = [], [], [], []
                    for c in range(groups):
                        u_c = wet_a[c] * u[c] + wet_b[c] * v[c] - wet_c[c] * (after[c] - before[c])
                        v_c = wet_a[c] * v[c] - wet_b[c] * u[c] - wet_c[c] * slope[c]
                        u_new.append(u_c)
                        v_new.append(v_c)
                        along.append(depth[c] * u_c + h[c] * mu[c])
                        cross.append(depth[c] * v_c + h[c] * mv[c])
                    cross = lane_steps(cross, lane)
                    part = [h[c] - cross[c] for c in range(groups)]
                    stores += [
                        (dst, 3 * layer, r, kg, part),
                        (dst, 3 * layer + 1, r, kg, u_new),
                        (dst, 3 * layer + 2, r, kg, v_new),
                        (flux, layer, r, kg, along),
                    ]
        for store in stores:
            put(*store)

    def rise(t, dst, r_first, count):
        stores = []
        for r in [r_first + k for k in range(count)]:
            g = first_row - DEPTH + r
            keep = jnp.where(jnp.logical_and(g >= 0, g < grid_rows), 1.0, 0.0).astype(f32)
            for kg in halves:
                fresh = []
                for layer in range(2):
                    part = at(dst, 3 * layer, r, kg)
                    before, after = at(flux, layer, r - 1, kg), at(flux, layer, r + 1, kg)
                    fresh.append(
                        [keep * (part[c] - (after[c] - before[c])) for c in range(groups)]
                    )
                    stores.append((dst, 3 * layer, r, kg, fresh[-1]))
                if t < ITERS - 1:
                    both = [press_of(fresh[0][c], fresh[1][c]) for c in range(groups)]
                    for layer in range(2):
                        stores.append((press, layer, r, kg, [p[layer] for p in both]))
        for store in stores:
            put(*store)

    src, dst = state_a, state_b
    for t in range(ITERS):
        first = 2 * t + 1
        n_move = ext - 4 * t - 2
        pace = 2 if n_move % 2 == 0 else 1

        def move_body(i, carry, t=t, src=src, dst=dst, first=first, pace=pace):
            move(t, src, dst, first + pace * i, pace)
            return carry

        lax.fori_loop(0, n_move // pace, move_body, 0)
        n_rise = n_move - 2
        pace_rise = 4 if n_rise % 4 == 0 else (2 if n_rise % 2 == 0 else 1)

        def rise_body(i, carry, t=t, dst=dst, first=first, pace=pace_rise):
            rise(t, dst, first + 1 + pace * i, pace)
            return carry

        lax.fori_loop(0, n_rise // pace_rise, rise_body, 0)
        src, dst = dst, src

    n_stations = stations_ref.shape[1]
    total = jnp.zeros((3 * GROUP, n_stations), f32)
    for r in range(tile_rows):
        for f in range(6):
            pf_out[f, r] = src[f, DEPTH + r].astype(bf16)
        surface = src[0, DEPTH + r] + src[3, DEPTH + r]
        high = surface.astype(bf16)
        rest = surface - high.astype(f32)
        middle = rest.astype(bf16)
        low = (rest - middle.astype(f32)).astype(bf16)
        pieces = jnp.concatenate([high, middle, low], axis=0)
        hits = station_hits(stations_ref, r, cells).astype(f32).astype(bf16)
        total = total + jnp.dot(pieces, hits, preferred_element_type=f32)
    sensed_out[...] = (
        total[:GROUP] + (total[GROUP : 2 * GROUP] + total[2 * GROUP : 3 * GROUP])
    )


def gram_kernel(where_ref, weight_ref, innov_ref, *refs, columns):
    sensed_refs, out_ref, both = refs[:-2], refs[-2], refs[-1]
    index = where_ref[1]
    count = len(sensed_refs)
    for d in range(count):
        start = pl.multiple_of(lax.rem(index + d, count) * columns, 8)
        both[pl.ds(start, columns), :] = sensed_refs[d][...] * weight_ref[...]
    total = count * columns
    both[pl.ds(total, 8), :] = innov_ref[...]
    out_ref[...] = lax.dot_general(
        both[...],
        both[pl.ds(0, total), :],
        (((1,), (1,)), ((), ())),
        precision=lax.Precision.HIGHEST,
        preferred_element_type=f32,
    )


def factor_kernel(where_ref, gram_ref, mix_out, scr, *, columns):
    index = where_ref[1]
    total = gram_ref.shape[1]
    blocks = total // 8
    lane = lax.broadcasted_iota(jnp.int32, (8, total), 1)
    sub = lax.broadcasted_iota(jnp.int32, (8, total), 0)
    eye = [(lane == sub + 8 * b).astype(f32) for b in range(blocks)]
    m = [gram_ref[pl.ds(8 * b, 8), :] + eye[b] for b in range(blocks)]
    w = list(eye)

    def column(x, j):
        return jnp.broadcast_to(x[:, j : j + 1], (8, total))

    def row(x, i):
        return jnp.broadcast_to(x[i : i + 1, :], (8, total))

    scaled = []
    for b in range(blocks):
        heads = [column(m[b], 8 * b + i) for i in range(8)]
        z_m, z_w, low = m[b], w[b], w[b]
        pivots = jnp.ones((8, total), f32)
        for i in range(8):
            pivot = row(heads[i], i)
            pivots = jnp.where(sub == i, pivot, pivots)
            inverse = 1.0 / pivot
            here = sub == i
            head = heads[i]
            for k in range(i + 1, 8):
                factor = row(heads[k], i) * inverse
                heads[k] = jnp.where(here, factor, heads[k] - head * factor)
            row_m = row(z_m, i) * inverse
            row_w = row(z_w, i) * inverse
            z_m = jnp.where(here, row_m, z_m - head * row_m)
            z_w = jnp.where(here, row_w, z_w - head * row_w)
            low = jnp.where(sub > i, low - head * row_w, low)
        scaled.append(low / jnp.sqrt(pivots))
        rows_m = [row(z_m, i) for i in range(8)]
        rows_w = [row(z_w, i) for i in range(8)]
        for q in range(b + 1, blocks):
            tails = [column(m[q], 8 * b + i) for i in range(8)]
            m[q] = m[q] - tree_sum([tails[i] * rows_m[i] for i in range(8)])
            w[q] = w[q] - tree_sum([tails[i] * rows_w[i] for i in range(8)])
    target = gram_ref[pl.ds(total, 1), :]
    weights = jnp.zeros((8, total), f32)
    for b in range(blocks):
        scr[pl.ds(8 * b, 8), :] = scaled[b]
        half = jnp.sum(scaled[b] * target, axis=1, keepdims=True)
        weights = weights + scaled[b] * half
    weights = jnp.sum(weights, axis=0, keepdims=True)
    shift = lax.rem(total - index * columns, total)
    mine = scr[pl.ds(pl.multiple_of(index * columns, 8), columns), :]
    mix_out[pl.ds(0, columns), :] = pltpu.roll(mine, shift, 1).astype(bf16)
    weights = pltpu.roll(jnp.broadcast_to(weights, (8, total)), shift, 1)
    high = weights.astype(bf16)
    low = (weights - high.astype(f32)).astype(bf16)
    pad = jnp.zeros((8, total), f32)
    rows = jnp.where(sub == 0, high.astype(f32), jnp.where(sub == 1, low.astype(f32), 0.0))
    mix_out[pl.ds(columns, 16), :] = jnp.concatenate([rows, pad], axis=0).astype(bf16)


def tree_sum(values):
    while len(values) > 1:
        values = [values[i] + values[i + 1] for i in range(0, len(values), 2)]
    return values[0]


def mix_kernel(where_ref, mix_ref, mean_ref, *refs, columns):
    piece_refs, cov_out, mean_out, scr = refs[:-3], refs[-3], refs[-2], refs[-1]
    tile_rows, cells = mean_ref.shape[1:]
    piece = mean_out.shape[2]
    group = pl.program_id(1)
    mix = mix_ref[...]
    cov_flat = cov_out.reshape(columns * tile_rows, 128)
    for r in range(tile_rows):
        stack = jnp.concatenate([ref[0, r] for ref in piece_refs], axis=0)
        result = jnp.dot(mix, stack, preferred_element_type=f32)
        cov_flat[pl.ds(r, columns, stride=tile_rows), :] = result[:columns]
        scr[group, pl.ds(r, 1), :] = (
            result[columns : columns + 1] + result[columns + 1 : columns + 2]
        )

    @pl.when(group == pl.num_programs(1) - 1)
    def _():
        change = jnp.concatenate([scr[c] for c in range(cells // 128)], axis=1)
        whole = mean_ref[0] + change
        shift = lax.rem(cells - where_ref[1] * piece, cells)
        mean_out[0] = pltpu.roll(whole, shift, 1)[:, :piece]


def spread_sum(value, axis):
    count = lax.axis_size(axis)
    if count & (count - 1):
        return lax.psum(value, axis)
    step = 1
    while step < count:
        value = value + lax.ppermute(value, axis, [(i, i ^ step) for i in range(count)])
        step *= 2
    return value


def shifted(value, axis):
    count = lax.axis_size(axis)
    return [value] + [
        lax.ppermute(value, axis, [((i + d) % count, i) for i in range(count)])
        for d in range(1, count)
    ]


def whole_spec(shape):
    return pl.BlockSpec(shape, lambda *_: (0,) * len(shape))


def local(mean_state, covariance, land_mask, stations, observed, obs_weight):
    columns, _, tile_rows, cells = covariance.shape
    piece = mean_state.shape[2]
    n_space = lax.axis_size("space")
    n_cols = lax.axis_size("cols")
    total = columns * n_cols
    grid_rows = tile_rows * n_space
    ext = tile_rows + 2 * DEPTH
    n_stations = stations.shape[0]
    chunks = columns // GROUP
    n_halo = len(halo_rows())
    groups = cells // 128
    space_index = lax.axis_index("space")
    column_index = lax.axis_index("cols")
    first_row = space_index * tile_rows
    where = jnp.stack([first_row, column_index]).astype(jnp.int32)
    up = [(i, i + 1) for i in range(n_space - 1)]
    down = [(i + 1, i) for i in range(n_space - 1)]
    smem = pl.BlockSpec(memory_space=pltpu.SMEM)

    mean_low = lax.ppermute(mean_state[:, tile_rows - DEPTH :, :], "space", up)
    mean_high = lax.ppermute(mean_state[:, :DEPTH, :], "space", down)
    mean_ext = jnp.concatenate([mean_low, mean_state, mean_high], axis=1)
    mean_ext = lax.all_gather(mean_ext, "cols", axis=2, tiled=True)

    flat = covariance.reshape(columns * 6 * tile_rows, cells)
    span = GROUP * 6 * tile_rows


    def cov_specs(c):
        return [pl.BlockSpec((span, 128), lambda i, g=g: (c, g)) for g in range(groups)]

    lows, highs = [], []
    for c in range(chunks):
        halo_shape = jax.ShapeDtypeStruct((n_halo, GROUP, cells), bf16)
        going_up, going_down = pl.pallas_call(
            functools.partial(pack_kernel, tile_rows=tile_rows),
            grid=(1,),
            in_specs=cov_specs(c),
            out_specs=[whole_spec((n_halo, GROUP, cells))] * 2,
            out_shape=[halo_shape, halo_shape],
            name=f"pack_{c}",
        )(*[flat] * groups)
        lows.append(lax.ppermute(going_up, "space", up))
        highs.append(lax.ppermute(going_down, "space", down))

    station_row = (stations - first_row * cells).astype(jnp.int32)[None, :]
    weight_row = obs_weight[None, :]
    wet, coef, mean_final, innovation = pl.pallas_call(
        functools.partial(mean_kernel, tile_rows=tile_rows, grid_rows=grid_rows),
        in_specs=[smem] + [pl.BlockSpec(memory_space=pltpu.VMEM)] * 5,
        out_specs=[pl.BlockSpec(memory_space=pltpu.VMEM)] * 4,
        out_shape=[
            jax.ShapeDtypeStruct((groups * 3 * ext, 128), f32),
            jax.ShapeDtypeStruct((groups * ITERS * 6 * ext, 128), f32),
            jax.ShapeDtypeStruct((6, tile_rows, cells), f32),
            jax.ShapeDtypeStruct((8, n_stations), f32),
        ],
        name="mean_window",
    )(where, mean_ext, land_mask, station_row, observed[None, :], weight_row)

    forecasts, sensed = [], []
    for c in range(chunks):
        pf, s = pl.pallas_call(
            functools.partial(window_kernel, tile_rows=tile_rows, grid_rows=grid_rows),
            grid=(1,),
            in_specs=[
                smem,
                whole_spec((n_halo, GROUP, cells)),
                whole_spec((n_halo, GROUP, cells)),
                whole_spec((groups * 3 * ext, 128)),
                whole_spec((groups * ITERS * 6 * ext, 128)),
                whole_spec((1, n_stations)),
            ]
            + cov_specs(c),
            out_specs=[
                whole_spec((6, tile_rows, GROUP, cells)),
                whole_spec((GROUP, n_stations)),
            ],
            out_shape=[
                jax.ShapeDtypeStruct((6, tile_rows, GROUP, cells), bf16),
                jax.ShapeDtypeStruct((GROUP, n_stations), f32),
            ],
            scratch_shapes=[pltpu.VMEM((n, ext, GROUP, cells), f32) for n in (6, 6, 2, 2)],
            name=f"window_{c}",
        )(where, lows[c], highs[c], wet, coef, station_row, *[flat] * groups)
        forecasts.append(shifted(pf, "cols"))
        sensed.append(s)

    sensed_all = shifted(jnp.concatenate(sensed, axis=0), "cols")
    gram = pl.pallas_call(
        functools.partial(gram_kernel, columns=columns),
        in_specs=[smem] + [pl.BlockSpec(memory_space=pltpu.VMEM)] * (2 + n_cols),
        out_specs=pl.BlockSpec(memory_space=pltpu.VMEM),
        out_shape=jax.ShapeDtypeStruct((total + 8, total), f32),
        scratch_shapes=[pltpu.VMEM((total + 8, n_stations), f32)],
        name="gram",
    )(where, weight_row, innovation, *sensed_all)
    gram = spread_sum(gram, "space")
    mix = pl.pallas_call(
        functools.partial(factor_kernel, columns=columns),
        in_specs=[smem, pl.BlockSpec(memory_space=pltpu.VMEM)],
        out_specs=pl.BlockSpec(memory_space=pltpu.VMEM),
        out_shape=jax.ShapeDtypeStruct((columns + 16, total), bf16),
        scratch_shapes=[pltpu.VMEM((total, total), f32)],
        name="factor",
    )(where, gram)

    pieces = [forecasts[c][d] for d in range(n_cols) for c in range(chunks)]
    field_spec = pl.BlockSpec((1, tile_rows, GROUP, 128), lambda f, g: (f, 0, 0, g))
    updated, mean_out = pl.pallas_call(
        functools.partial(mix_kernel, columns=columns),
        grid=(6, groups),
        in_specs=[
            smem,
            whole_spec((columns + 16, total)),
            pl.BlockSpec((1, tile_rows, cells), lambda f, g: (f, 0, 0)),
        ]
        + [field_spec] * len(pieces),
        out_specs=[
            pl.BlockSpec((columns, 1, tile_rows, 128), lambda f, g: (0, f, 0, g)),
            pl.BlockSpec((1, tile_rows, piece), lambda f, g: (f, 0, 0)),
        ],
        out_shape=[
            jax.ShapeDtypeStruct((columns, 6, tile_rows, cells), f32),
            jax.ShapeDtypeStruct((6, tile_rows, piece), f32),
        ],
        scratch_shapes=[pltpu.VMEM((groups, tile_rows, 128), f32)],
        name="mix",
    )(where, mix, mean_final, *pieces)
    return (mean_out, updated)


def solution(mesh):
    return jax.shard_map(
        local,
        mesh=mesh,
        in_specs=(
            P(None, "space", "cols"),
            P("cols", None, "space", None),
            P(),
            P("space"),
            P("space"),
            P("space"),
        ),
        out_specs=(P(None, "space", "cols"), P("cols", None, "space", None)),
        check_vma=False,
    )
```

```python
import functools

import jax
import jax.numpy as jnp
from jax import lax
from jax.experimental import pallas as pl
from jax.experimental.pallas import tpu as pltpu
from jax.sharding import PartitionSpec as P


ITERS = 4
DEPTH = 2 * ITERS
GROUP = 16

time_step = 0.5
gravity = 1.0
reduced_gravity = 0.125
coriolis = 0.3
friction = 0.05
layer_depths = (1.0, 2.0)

keep_part = 1.0 - time_step * friction
turn_part = time_step * coriolis
slope_part = 0.5 * time_step

f32 = jnp.float32
bf16 = jnp.bfloat16


def halo_rows():
    rows = []
    for layer in range(2):
        rows += [(3 * layer, d) for d in range(DEPTH, 0, -1)]
    for layer in range(2):
        rows += [(3 * layer + 1, d) for d in range(DEPTH - 1, 0, -1)]
        rows += [(3 * layer + 2, d) for d in range(DEPTH - 2, 0, -1)]
    return rows


def turn(src_ref, src_row, stride, turned, base, tile_rows):
    pitch = GROUP + 1
    for k in range(GROUP):
        for r in range(0, tile_rows, 8):
            turned[pl.ds(base + r * pitch + k, 8, stride=pitch), :] = src_ref[
                pl.ds(k * stride + src_row + r, 8), :
            ]


def turned_row(turned, base, r):
    pitch = GROUP + 1
    return jnp.concatenate(
        [turned[pl.ds(base + r * pitch + 8 * kg, 8, stride=1), :] for kg in range(GROUP // 8)],
        axis=0,
    )


def turned_size(tile_rows):
    return tile_rows * (GROUP + 1) + 8


def pack_kernel(*refs, tile_rows):
    cov_refs, (up_ref, down_ref, turned) = refs[:-3], refs[-3:]
    stride = 6 * tile_rows
    size = turned_size(tile_rows)
    groups = len(cov_refs)
    for f in range(6):
        for c in range(groups):
            turn(cov_refs[c], f * tile_rows, stride, turned, (f * groups + c) * size, tile_rows)

    def row(field, r):
        return jnp.concatenate(
            [turned_row(turned, (field * groups + c) * size, r) for c in range(groups)], axis=1
        )

    for i, (field, d) in enumerate(halo_rows()):
        for ref, r in ((up_ref, tile_rows - d), (down_ref, d - 1)):
            value = row(field, r)
            if d == DEPTH - 1 and field % 3 == 1:
                value = value + (turn_part / keep_part) * row(field + 1, r)
            ref[i] = value.astype(bf16)


def lane_steps(parts, lane):
    n = len(parts)
    right = [pltpu.roll(p, 1, 1) for p in parts]
    left = [pltpu.roll(p, 127, 1) for p in parts]
    out = []
    for i in range(n):
        before = jnp.where(lane == 0, right[i - 1] if i > 0 else 0.0, right[i])
        after = jnp.where(lane == 127, left[i + 1] if i < n - 1 else 0.0, left[i])
        out.append(after - before)
    return out


def station_hits(stations_ref, r, cells):
    position = lax.broadcasted_iota(jnp.int32, (cells, stations_ref.shape[1]), 0) + r * cells
    return position == stations_ref[...]


def mean_kernel(
    where_ref, mean_ref, mask_ref, stations_ref, observed_ref, weight_ref,
    wet_out, coef_out, final_out, innov_out, *, tile_rows, grid_rows,
):
    first_row = where_ref[0]
    ext, cells = mean_ref.shape[1:]
    wets = []
    for i in range(ext // 8):
        g = first_row - DEPTH + 8 * i
        inside = jnp.logical_and(g >= 0, g < grid_rows).astype(f32)
        start = pl.multiple_of(jnp.clip(g, 0, grid_rows - 8), 8)
        wets.append(mask_ref[pl.ds(start, 8), :].astype(f32) * inside)
    wet = jnp.concatenate(wets, axis=0)
    g_all = first_row - DEPTH + lax.broadcasted_iota(jnp.int32, (ext, cells), 0)
    keep = jnp.logical_and(g_all >= 0, g_all < grid_rows).astype(f32)
    lane_all = lax.broadcasted_iota(jnp.int32, (ext, cells), 1)

    def put(ref, index, value):
        rows = ref.shape[0] // (cells // 128)
        for c in range(cells // 128):
            ref[pl.ds(c * rows + index * ext, ext), :] = value[:, 128 * c : 128 * c + 128]

    put(wet_out, 0, wet * keep_part)
    put(wet_out, 1, wet * turn_part)
    put(wet_out, 2, wet * slope_part)

    def diff_rows(a):
        return 0.5 * (pltpu.roll(a, ext - 1, 0) - pltpu.roll(a, 1, 0))

    def diff_cols(a):
        after = jnp.where(lane_all == cells - 1, 0.0, pltpu.roll(a, cells - 1, 1))
        before = jnp.where(lane_all == 0, 0.0, pltpu.roll(a, 1, 1))
        return 0.5 * (after - before)

    state = [mean_ref[f] for f in range(6)]
    for t in range(ITERS):
        pressure_top = gravity * (state[0] + state[3])
        pressures = (pressure_top, pressure_top - reduced_gravity * state[0])
        fresh = []
        for layer in range(2):
            h, u, v = state[3 * layer : 3 * layer + 3]
            p = pressures[layer]
            u_new = wet * (u + time_step * (-diff_rows(p) + coriolis * v - friction * u))
            v_new = wet * (v + time_step * (-diff_cols(p) - coriolis * u - friction * v))
            depth = layer_depths[layer] + h
            h_new = h - time_step * (diff_rows(depth * u_new) + diff_cols(depth * v_new))
            for q, value in enumerate((depth, u_new, v_new)):
                put(coef_out, t * 6 + 3 * layer + q, slope_part * value)
            fresh += [h_new * keep, u_new, v_new]
        state = fresh
    for f in range(6):
        final_out[f] = state[f][DEPTH : DEPTH + tile_rows, :]
    surface = (state[0] + state[3])[DEPTH : DEPTH + tile_rows, :]
    n_stations = stations_ref.shape[1]
    sublane = lax.broadcasted_iota(jnp.int32, (8, n_stations), 0)
    picked = jnp.zeros((8, n_stations), f32)
    for r in range(tile_rows):
        hits = station_hits(stations_ref, r, cells).astype(f32)
        block = surface[r // 8 * 8 : r // 8 * 8 + 8, :]
        values = jnp.dot(block, hits, precision=lax.Precision.HIGHEST, preferred_element_type=f32)
        picked = picked + jnp.where(sublane == r % 8, values, 0.0)
    at_station = jnp.sum(picked, axis=0, keepdims=True)
    innovation = weight_ref[...] * (observed_ref[...] - at_station)
    innov_out[...] = jnp.where(sublane == 0, innovation, 0.0)


def window_kernel(
    where_ref, low_ref, high_ref, wet_ref, coef_ref, stations_ref, *refs,
    tile_rows, grid_rows,
):
    cov_refs, (pf_out, sensed_out, state_a, state_b, press, flux, turned) = refs[:-7], refs[-7:]
    first_row = where_ref[0]
    ext = tile_rows + 2 * DEPTH
    groups = len(cov_refs)
    cells = 128 * groups
    stride = 6 * tile_rows
    halves = range(GROUP // 8)

    def at(ref, field, r, kg):
        return [ref[field, r, pl.ds(8 * kg, 8), pl.ds(128 * c, 128)] for c in range(groups)]

    def put(ref, field, r, kg, parts):
        for c in range(groups):
            ref[field, r, pl.ds(8 * kg, 8), pl.ds(128 * c, 128)] = parts[c]

    def spread(ref, index, r):
        rows = ref.shape[0] // groups
        return [ref[pl.ds(c * rows + index * ext + r, 8, stride=0), :] for c in range(groups)]

    size = turned_size(tile_rows)
    for f in range(6):
        for c in range(groups):
            base = (f * groups + c) * size
            turn(cov_refs[c], f * tile_rows, stride, turned, base, tile_rows)
            for r in range(tile_rows):
                state_a[f, DEPTH + r, :, pl.ds(128 * c, 128)] = turned_row(turned, base, r)
    for i, (field, d) in enumerate(halo_rows()):
        state_a[field, DEPTH - d] = low_ref[i].astype(f32)
        state_a[field, DEPTH + tile_rows + d - 1] = high_ref[i].astype(f32)
    for layer in range(2):
        for r in (1, ext - 2):
            state_a[3 * layer + 2, r] = jnp.zeros((GROUP, cells), f32)

    def press_of(top, bottom):
        p_top = gravity * (top + bottom)
        return p_top, p_top - reduced_gravity * top

    def first_press(r, carry):
        press[0, r], press[1, r] = press_of(state_a[0, r], state_a[3, r])
        return carry

    lax.fori_loop(0, ext, first_press, 0, unroll=2)
    lane = lax.broadcasted_iota(jnp.int32, (8, 128), 1)

    def move(t, src, dst, r_first, count, edge=False):
        stores = []
        for r in [r_first + k for k in range(count)]:
            wet_a, wet_b, wet_c = (spread(wet_ref, q, r) for q in range(3))
            for layer in range(2):
                depth, mu, mv = (spread(coef_ref, t * 6 + 3 * layer + q, r) for q in range(3))
                for kg in halves:
                    h = at(src, 3 * layer, r, kg)
                    u = at(src, 3 * layer + 1, r, kg)
                    v = at(src, 3 * layer + 2, r, kg)
                    before = at(press, layer, r - 1, kg)
                    after = at(press, layer, r + 1, kg)
                    if edge:
                        u_new, along = [], []
                        for c in range(groups):
                            u_c = (
                                wet_a[c] * u[c] + wet_b[c] * v[c] - wet_c[c] * (after[c] - before[c])
                            )
                            along.append(depth[c] * u_c + h[c] * mu[c])
                        stores.append((flux, layer, r, kg, along))
                        continue
                    slope = lane_steps(at(press, layer, r, kg), lane)
                    u_new, v_new, along, cross = [], [], [], []
                    for c in range(groups):
                        u_c = wet_a[c] * u[c] + wet_b[c] * v[c] - wet_c[c] * (after[c] - before[c])
                        v_c = wet_a[c] * v[c] - wet_b[c] * u[c] - wet_c[c] * slope[c]
                        u_new.append(u_c)
                        v_new.append(v_c)
                        along.append(depth[c] * u_c + h[c] * mu[c])
                        cross.append(depth[c] * v_c + h[c] * mv[c])
                    cross = lane_steps(cross, lane)
                    part = [h[c] - cross[c] for c in range(groups)]
                    stores += [
                        (dst, 3 * layer, r, kg, part),
                        (dst, 3 * layer + 1, r, kg, u_new),
                        (dst, 3 * layer + 2, r, kg, v_new),
                        (flux, layer, r, kg, along),
                    ]
        for store in stores:
            put(*store)

    def rise(t, dst, r_first, count):
        stores = []
        for r in [r_first + k for k in range(count)]:
            g = first_row - DEPTH + r
            keep = jnp.where(jnp.logical_and(g >= 0, g < grid_rows), 1.0, 0.0).astype(f32)
            for kg in halves:
                fresh = []
                for layer in range(2):
                    part = at(dst, 3 * layer, r, kg)
                    before, after = at(flux, layer, r - 1, kg), at(flux, layer, r + 1, kg)
                    fresh.append(
                        [keep * (part[c] - (after[c] - before[c])) for c in range(groups)]
                    )
                    stores.append((dst, 3 * layer, r, kg, fresh[-1]))
                if t < ITERS - 1:
                    both = [press_of(fresh[0][c], fresh[1][c]) for c in range(groups)]
                    for layer in range(2):
                        stores.append((press, layer, r, kg, [p[layer] for p in both]))
        for store in stores:
            put(*store)

    src, dst = state_a, state_b
    for t in range(ITERS):
        first = 2 * t + 2
        rows = ext - 4 * t - 4
        pace = 4 if rows % 4 == 0 else (2 if rows % 2 == 0 else 1)
        move(t, src, dst, first - 1, 1, edge=True)
        move(t, src, dst, first + rows, 1, edge=True)

        def move_body(i, carry, t=t, src=src, dst=dst, first=first, pace=pace):
            move(t, src, dst, first + pace * i, pace)
            return carry

        lax.fori_loop(0, rows // pace, move_body, 0)

        def rise_body(i, carry, t=t, dst=dst, first=first, pace=pace):
            rise(t, dst, first + pace * i, pace)
            return carry

        lax.fori_loop(0, rows // pace, rise_body, 0)
        src, dst = dst, src

    n_stations = stations_ref.shape[1]
    total = jnp.zeros((3 * GROUP, n_stations), f32)
    for r in range(tile_rows):
        for f in range(6):
            pf_out[f, r] = src[f, DEPTH + r].astype(bf16)
        surface = src[0, DEPTH + r] + src[3, DEPTH + r]
        high = surface.astype(bf16)
        rest = surface - high.astype(f32)
        middle = rest.astype(bf16)
        low = (rest - middle.astype(f32)).astype(bf16)
        pieces = jnp.concatenate([high, middle, low], axis=0)
        hits = station_hits(stations_ref, r, cells).astype(f32).astype(bf16)
        total = total + jnp.dot(pieces, hits, preferred_element_type=f32)
    sensed_out[...] = (
        total[:GROUP] + (total[GROUP : 2 * GROUP] + total[2 * GROUP : 3 * GROUP])
    )


def gram_kernel(where_ref, weight_ref, innov_ref, *refs, columns):
    sensed_refs, out_ref, both, left = refs[:-3], refs[-3], refs[-2], refs[-1]
    index = where_ref[1]
    count = both.shape[0] // columns
    each = len(sensed_refs) // count
    for d in range(count):
        start = pl.multiple_of(lax.rem(index + d, count) * columns, 8)
        for ref in sensed_refs[d * each : (d + 1) * each]:
            size = ref.shape[0]
            both[pl.ds(start, size), :] = ref[...] * weight_ref[...]
            start = pl.multiple_of(start + size, 8)
    left[pl.ds(0, columns), :] = both[pl.ds(pl.multiple_of(index * columns, 8), columns), :]
    left[pl.ds(columns, 8), :] = innov_ref[...]
    out_ref[...] = lax.dot_general(
        left[...],
        both[...],
        (((1,), (1,)), ((), ())),
        precision=lax.Precision.HIGHEST,
        preferred_element_type=f32,
    )


def factor_kernel(where_ref, *refs, columns):
    gram_refs, mix_out, scr = refs[:-2], refs[-2], refs[-1]
    index = where_ref[1]
    count = len(gram_refs)
    total = count * columns
    for d in range(count):
        start = pl.multiple_of(lax.rem(index + d, count) * columns, 8)
        scr[pl.ds(start, columns), :] = gram_refs[d][pl.ds(0, columns), :]
    blocks = total // 8
    lane = lax.broadcasted_iota(jnp.int32, (8, total), 1)
    sub = lax.broadcasted_iota(jnp.int32, (8, total), 0)
    eye = [(lane == sub + 8 * b).astype(f32) for b in range(blocks)]
    m = [scr[pl.ds(8 * b, 8), :] + eye[b] for b in range(blocks)]
    w = list(eye)

    def column(x, j):
        return jnp.broadcast_to(x[:, j : j + 1], (8, total))

    def row(x, i):
        return jnp.broadcast_to(x[i : i + 1, :], (8, total))

    scaled = []
    for b in range(blocks):
        heads = [column(m[b], 8 * b + i) for i in range(8)]
        z_m, z_w, low = m[b], w[b], w[b]
        pivots = jnp.ones((8, total), f32)
        for i in range(8):
            pivot = row(heads[i], i)
            pivots = jnp.where(sub == i, pivot, pivots)
            inverse = 1.0 / pivot
            here = sub == i
            head = heads[i]
            for k in range(i + 1, 8):
                factor = row(heads[k], i) * inverse
                heads[k] = jnp.where(here, factor, heads[k] - head * factor)
            row_m = row(z_m, i) * inverse
            row_w = row(z_w, i) * inverse
            z_m = jnp.where(here, row_m, z_m - head * row_m)
            z_w = jnp.where(here, row_w, z_w - head * row_w)
            low = jnp.where(sub > i, low - head * row_w, low)
        scaled.append(low / jnp.sqrt(pivots))
        rows_m = [row(z_m, i) for i in range(8)]
        rows_w = [row(z_w, i) for i in range(8)]
        for q in range(b + 1, blocks):
            tails = [column(m[q], 8 * b + i) for i in range(8)]
            m[q] = m[q] - tree_sum([tails[i] * rows_m[i] for i in range(8)])
            w[q] = w[q] - tree_sum([tails[i] * rows_w[i] for i in range(8)])
    target = gram_refs[0][pl.ds(columns, 1), :]
    weights = jnp.zeros((8, total), f32)
    for b in range(blocks):
        scr[pl.ds(8 * b, 8), :] = scaled[b]
        half = jnp.sum(scaled[b] * target, axis=1, keepdims=True)
        weights = weights + scaled[b] * half
    weights = jnp.sum(weights, axis=0, keepdims=True)
    shift = lax.rem(total - index * columns, total)
    mine = scr[pl.ds(pl.multiple_of(index * columns, 8), columns), :]
    mix_out[pl.ds(0, columns), :] = pltpu.roll(mine, shift, 1).astype(bf16)
    weights = pltpu.roll(jnp.broadcast_to(weights, (8, total)), shift, 1)
    high = weights.astype(bf16)
    low = (weights - high.astype(f32)).astype(bf16)
    pad = jnp.zeros((8, total), f32)
    rows = jnp.where(sub == 0, high.astype(f32), jnp.where(sub == 1, low.astype(f32), 0.0))
    mix_out[pl.ds(columns, 16), :] = jnp.concatenate([rows, pad], axis=0).astype(bf16)


def tree_sum(values):
    while len(values) > 1:
        values = [values[i] + values[i + 1] for i in range(0, len(values), 2)]
    return values[0]


def mix_kernel(where_ref, mix_ref, mean_ref, *refs, columns):
    piece_refs, (cov_out, mean_out, scr, turned) = refs[:-4], refs[-4:]
    tile_rows, cells = mean_ref.shape[1:]
    groups = cells // 128
    piece = mean_out.shape[2]
    mix = mix_ref[...]
    pitch = tile_rows + 1
    for r in range(tile_rows):
        stack = jnp.concatenate([ref[0, r] for ref in piece_refs], axis=0)
        result = jnp.dot(mix, stack, preferred_element_type=f32)
        for c in range(groups):
            for j in range(0, columns, 8):
                turned[c, pl.ds(j * pitch + r, 8, stride=pitch), :] = result[
                    j : j + 8, 128 * c : 128 * c + 128
                ]
        scr[pl.ds(r, 1), :] = result[columns : columns + 1] + result[columns + 1 : columns + 2]
    for j in range(columns):
        for c in range(groups):
            for r in range(0, tile_rows, 8):
                cov_out[j, 0, pl.ds(r, 8), pl.ds(128 * c, 128)] = turned[
                    c, pl.ds(j * pitch + r, 8, stride=1), :
                ]
    whole = mean_ref[0] + scr[...]
    shift = lax.rem(cells - where_ref[1] * piece, cells)
    mean_out[0] = pltpu.roll(whole, shift, 1)[:, :piece]


def spread_sum(value, axis):
    count = lax.axis_size(axis)
    if count & (count - 1):
        return lax.psum(value, axis)
    step = 1
    while step < count:
        value = value + lax.ppermute(value, axis, [(i, i ^ step) for i in range(count)])
        step *= 2
    return value


def shifted(value, axis):
    count = lax.axis_size(axis)
    return [value] + [
        lax.ppermute(value, axis, [((i + d) % count, i) for i in range(count)])
        for d in range(1, count)
    ]


def whole_spec(shape):
    return pl.BlockSpec(shape, lambda *_: (0,) * len(shape))


def chunk_list(count):
    if count < 3:
        return [(g, 1) for g in range(count)]
    return [(0, 1), (1, count - 2), (count - 1, 1)]


def local(mean_state, covariance, land_mask, stations, observed, obs_weight):
    columns, _, tile_rows, cells = covariance.shape
    piece = mean_state.shape[2]
    n_space = lax.axis_size("space")
    n_cols = lax.axis_size("cols")
    total = columns * n_cols
    grid_rows = tile_rows * n_space
    ext = tile_rows + 2 * DEPTH
    n_stations = stations.shape[0]
    chunks = chunk_list(columns // GROUP)
    n_halo = len(halo_rows())
    groups = cells // 128
    space_index = lax.axis_index("space")
    column_index = lax.axis_index("cols")
    first_row = space_index * tile_rows
    where = jnp.stack([first_row, column_index]).astype(jnp.int32)
    up = [(i, i + 1) for i in range(n_space - 1)]
    down = [(i + 1, i) for i in range(n_space - 1)]
    smem = pl.BlockSpec(memory_space=pltpu.SMEM)

    mean_low = lax.ppermute(mean_state[:, tile_rows - DEPTH :, :], "space", up)
    mean_high = lax.ppermute(mean_state[:, :DEPTH, :], "space", down)
    mean_ext = jnp.concatenate([mean_low, mean_state, mean_high], axis=1)
    mean_ext = lax.all_gather(mean_ext, "cols", axis=2, tiled=True)

    flat = covariance.reshape(columns * 6 * tile_rows, cells)
    span = GROUP * 6 * tile_rows


    def cov_specs(start):
        return [pl.BlockSpec((span, 128), lambda i, g=g: (start + i, g)) for g in range(groups)]

    halo_spec = pl.BlockSpec((n_halo, GROUP, cells), lambda i: (0, i, 0))
    lows, highs = [], []
    source = flat
    for start, size in chunks:
        halo_shape = jax.ShapeDtypeStruct((n_halo, size * GROUP, cells), bf16)
        going_up, going_down = pl.pallas_call(
            functools.partial(pack_kernel, tile_rows=tile_rows),
            grid=(size,),
            in_specs=cov_specs(start),
            out_specs=[halo_spec] * 2,
            out_shape=[halo_shape, halo_shape],
            scratch_shapes=[pltpu.VMEM((6 * groups * turned_size(tile_rows), 128), f32)],
        )(*[source] * groups)
        source, going_up, going_down = lax.optimization_barrier((flat, going_up, going_down))
        lows.append(lax.ppermute(going_up, "space", up))
        highs.append(lax.ppermute(going_down, "space", down))

    station_row = (stations - first_row * cells).astype(jnp.int32)[None, :]
    weight_row = obs_weight[None, :]
    mean_run = pl.pallas_call(
        functools.partial(mean_kernel, tile_rows=tile_rows, grid_rows=grid_rows),
        in_specs=[smem] + [pl.BlockSpec(memory_space=pltpu.VMEM)] * 5,
        out_specs=[pl.BlockSpec(memory_space=pltpu.VMEM)] * 4,
        out_shape=[
            jax.ShapeDtypeStruct((groups * 3 * ext, 128), f32),
            jax.ShapeDtypeStruct((groups * ITERS * 6 * ext, 128), f32),
            jax.ShapeDtypeStruct((6, tile_rows, cells), f32),
            jax.ShapeDtypeStruct((8, n_stations), f32),
        ],
        name="mean_window",
    )
    wet, coef, mean_final, innovation = mean_run(
        where, mean_ext, land_mask, station_row, observed[None, :], weight_row
    )

    forecasts, sensed = [], []
    for c, (start, size) in enumerate(chunks):
        window = pl.pallas_call(
            functools.partial(window_kernel, tile_rows=tile_rows, grid_rows=grid_rows),
            grid=(size,),
            in_specs=[
                smem,
                halo_spec,
                halo_spec,
                whole_spec((groups * 3 * ext, 128)),
                whole_spec((groups * ITERS * 6 * ext, 128)),
                whole_spec((1, n_stations)),
            ]
            + cov_specs(start),
            out_specs=[
                pl.BlockSpec((6, tile_rows, GROUP, cells), lambda i: (0, 0, i, 0)),
                pl.BlockSpec((GROUP, n_stations), lambda i: (i, 0)),
            ],
            out_shape=[
                jax.ShapeDtypeStruct((6, tile_rows, size * GROUP, cells), bf16),
                jax.ShapeDtypeStruct((size * GROUP, n_stations), f32),
            ],
            scratch_shapes=[pltpu.VMEM((n, ext, GROUP, cells), f32) for n in (6, 6, 2, 2)]
            + [pltpu.VMEM((6 * groups * turned_size(tile_rows), 128), f32)],
        )
        pf, s = window(where, lows[c], highs[c], wet, coef, station_row, *[flat] * groups)
        forecasts.append(shifted(pf, "cols"))
        sensed.append(shifted(s, "cols"))

    sensed_all = [sensed[c][d] for d in range(n_cols) for c in range(len(chunks))]
    gram = pl.pallas_call(
        functools.partial(gram_kernel, columns=columns),
        in_specs=[smem] + [pl.BlockSpec(memory_space=pltpu.VMEM)] * (2 + len(sensed_all)),
        out_specs=pl.BlockSpec(memory_space=pltpu.VMEM),
        out_shape=jax.ShapeDtypeStruct((columns + 8, total), f32),
        scratch_shapes=[
            pltpu.VMEM((total, n_stations), f32),
            pltpu.VMEM((columns + 8, n_stations), f32),
        ],
        name="gram",
    )(where, weight_row, innovation, *sensed_all)
    gram_all = shifted(spread_sum(gram, "space"), "cols")
    mix = pl.pallas_call(
        functools.partial(factor_kernel, columns=columns),
        in_specs=[smem] + [pl.BlockSpec(memory_space=pltpu.VMEM)] * n_cols,
        out_specs=pl.BlockSpec(memory_space=pltpu.VMEM),
        out_shape=jax.ShapeDtypeStruct((columns + 16, total), bf16),
        scratch_shapes=[pltpu.VMEM((total, total), f32)],
        name="factor",
    )(where, *gram_all)

    pieces = [forecasts[c][d] for d in range(n_cols) for c in range(len(chunks))]
    updated, mean_out = pl.pallas_call(
        functools.partial(mix_kernel, columns=columns),
        grid=(6,),
        in_specs=[
            smem,
            whole_spec((columns + 16, total)),
            pl.BlockSpec((1, tile_rows, cells), lambda f: (f, 0, 0)),
        ]
        + [
            pl.BlockSpec((1, tile_rows, p.shape[2], cells), lambda f: (f, 0, 0, 0)) for p in pieces
        ],
        out_specs=[
            pl.BlockSpec((columns, 1, tile_rows, cells), lambda f: (0, f, 0, 0)),
            pl.BlockSpec((1, tile_rows, piece), lambda f: (f, 0, 0)),
        ],
        out_shape=[
            jax.ShapeDtypeStruct((columns, 6, tile_rows, cells), f32),
            jax.ShapeDtypeStruct((6, tile_rows, piece), f32),
        ],
        scratch_shapes=[
            pltpu.VMEM((tile_rows, cells), f32),
            pltpu.VMEM((groups, columns * (tile_rows + 1) + 8, 128), f32),
        ],
        name="mix",
    )(where, mix, mean_final, *pieces)
    return (mean_out, updated)


def solution(mesh):
    return jax.shard_map(
        local,
        mesh=mesh,
        in_specs=(
            P(None, "space", "cols"),
            P("cols", None, "space", None),
            P(),
            P("space"),
            P("space"),
            P("space"),
        ),
        out_specs=(P(None, "space", "cols"), P("cols", None, "space", None)),
        check_vma=False,
    )
```

```python
import functools

import jax
import jax.numpy as jnp
from jax import lax
from jax.experimental import pallas as pl
from jax.experimental.pallas import tpu as pltpu
from jax.sharding import PartitionSpec as P


ITERS = 4
DEPTH = 2 * ITERS
GROUP = 16

time_step = 0.5
gravity = 1.0
reduced_gravity = 0.125
coriolis = 0.3
friction = 0.05
layer_depths = (1.0, 2.0)

keep_part = 1.0 - time_step * friction
turn_part = time_step * coriolis
slope_part = 0.5 * time_step

f32 = jnp.float32
bf16 = jnp.bfloat16


def halo_rows():
    rows = []
    for layer in range(2):
        rows += [(3 * layer, d) for d in range(DEPTH, 0, -1)]
    for layer in range(2):
        rows += [(3 * layer + 1, d) for d in range(DEPTH - 1, 0, -1)]
        rows += [(3 * layer + 2, d) for d in range(DEPTH - 2, 0, -1)]
    return rows


def turn(src_ref, src_row, stride, turned, base, tile_rows):
    pitch = GROUP + 1
    for k in range(GROUP):
        for r in range(0, tile_rows, 8):
            turned[pl.ds(base + r * pitch + k, 8, stride=pitch), :] = src_ref[
                pl.ds(k * stride + src_row + r, 8), :
            ]


def turned_row(turned, base, r):
    pitch = GROUP + 1
    return jnp.concatenate(
        [turned[pl.ds(base + r * pitch + 8 * kg, 8, stride=1), :] for kg in range(GROUP // 8)],
        axis=0,
    )


def turned_size(tile_rows):
    return tile_rows * (GROUP + 1) + 8


def pack_kernel(*refs, tile_rows, with_mean):
    cov_refs, (up_ref, down_ref, turned) = refs[:-3], refs[-3:]
    if with_mean:
        mean_ref, cov_refs = cov_refs[0], cov_refs[1:]
        piece = mean_ref.shape[2]
        for i in range(3):
            for ref, r in ((up_ref, tile_rows - DEPTH), (down_ref, 0)):
                value = jnp.concatenate(
                    [mean_ref[f, pl.ds(r, DEPTH), :] for f in (2 * i, 2 * i + 1)], axis=0
                )
                high = value.astype(bf16)
                low = (value - high.astype(f32)).astype(bf16)
                ref[len(halo_rows()) + i, :, pl.ds(0, piece)] = high
                ref[len(halo_rows()) + i, :, pl.ds(128, piece)] = low
    stride = 6 * tile_rows
    size = turned_size(tile_rows)
    groups = len(cov_refs)
    for f in range(6):
        for c in range(groups):
            turn(cov_refs[c], f * tile_rows, stride, turned, (f * groups + c) * size, tile_rows)

    def row(field, r):
        return jnp.concatenate(
            [turned_row(turned, (field * groups + c) * size, r) for c in range(groups)], axis=1
        )

    for i, (field, d) in enumerate(halo_rows()):
        for ref, r in ((up_ref, tile_rows - d), (down_ref, d - 1)):
            value = row(field, r)
            if d == DEPTH - 1 and field % 3 == 1:
                value = value + (turn_part / keep_part) * row(field + 1, r)
            ref[i] = value.astype(bf16)


def lane_steps(parts, lane):
    n = len(parts)
    right = [pltpu.roll(p, 1, 1) for p in parts]
    left = [pltpu.roll(p, 127, 1) for p in parts]
    out = []
    for i in range(n):
        before = jnp.where(lane == 0, right[i - 1] if i > 0 else 0.0, right[i])
        after = jnp.where(lane == 127, left[i + 1] if i < n - 1 else 0.0, left[i])
        out.append(after - before)
    return out


def station_hits(stations_ref, r, cells):
    position = lax.broadcasted_iota(jnp.int32, (cells, stations_ref.shape[1]), 0) + r * cells
    return position == stations_ref[...]


def mean_kernel(
    where_ref, mean_ref, mask_ref, stations_ref, observed_ref, weight_ref,
    wet_out, coef_out, final_out, innov_out, *, tile_rows, grid_rows,
):
    first_row = where_ref[0]
    ext, cells = mean_ref.shape[1:]
    wets = []
    for i in range(ext // 8):
        g = first_row - DEPTH + 8 * i
        inside = jnp.logical_and(g >= 0, g < grid_rows).astype(f32)
        start = pl.multiple_of(jnp.clip(g, 0, grid_rows - 8), 8)
        wets.append(mask_ref[pl.ds(start, 8), :].astype(f32) * inside)
    wet = jnp.concatenate(wets, axis=0)
    g_all = first_row - DEPTH + lax.broadcasted_iota(jnp.int32, (ext, cells), 0)
    keep = jnp.logical_and(g_all >= 0, g_all < grid_rows).astype(f32)
    lane_all = lax.broadcasted_iota(jnp.int32, (ext, cells), 1)

    def put(ref, index, value):
        rows = ref.shape[0] // (cells // 128)
        for c in range(cells // 128):
            ref[pl.ds(c * rows + index * ext, ext), :] = value[:, 128 * c : 128 * c + 128]

    put(wet_out, 0, wet * keep_part)
    put(wet_out, 1, wet * turn_part)
    put(wet_out, 2, wet * slope_part)

    def diff_rows(a):
        return 0.5 * (pltpu.roll(a, ext - 1, 0) - pltpu.roll(a, 1, 0))

    def diff_cols(a):
        after = jnp.where(lane_all == cells - 1, 0.0, pltpu.roll(a, cells - 1, 1))
        before = jnp.where(lane_all == 0, 0.0, pltpu.roll(a, 1, 1))
        return 0.5 * (after - before)

    state = [mean_ref[f] for f in range(6)]
    for t in range(ITERS):
        pressure_top = gravity * (state[0] + state[3])
        pressures = (pressure_top, pressure_top - reduced_gravity * state[0])
        fresh = []
        for layer in range(2):
            h, u, v = state[3 * layer : 3 * layer + 3]
            p = pressures[layer]
            u_new = wet * (u + time_step * (-diff_rows(p) + coriolis * v - friction * u))
            v_new = wet * (v + time_step * (-diff_cols(p) - coriolis * u - friction * v))
            depth = layer_depths[layer] + h
            h_new = h - time_step * (diff_rows(depth * u_new) + diff_cols(depth * v_new))
            for q, value in enumerate((depth, u_new, v_new)):
                put(coef_out, t * 6 + 3 * layer + q, slope_part * value)
            fresh += [h_new * keep, u_new, v_new]
        state = fresh
    for f in range(6):
        final_out[f] = state[f][DEPTH : DEPTH + tile_rows, :]
    surface = (state[0] + state[3])[DEPTH : DEPTH + tile_rows, :]
    n_stations = stations_ref.shape[1]
    sublane = lax.broadcasted_iota(jnp.int32, (8, n_stations), 0)
    picked = jnp.zeros((8, n_stations), f32)
    for r in range(tile_rows):
        hits = station_hits(stations_ref, r, cells).astype(f32)
        block = surface[r // 8 * 8 : r // 8 * 8 + 8, :]
        values = jnp.dot(block, hits, precision=lax.Precision.HIGHEST, preferred_element_type=f32)
        picked = picked + jnp.where(sublane == r % 8, values, 0.0)
    at_station = jnp.sum(picked, axis=0, keepdims=True)
    innovation = weight_ref[...] * (observed_ref[...] - at_station)
    innov_out[...] = jnp.where(sublane == 0, innovation, 0.0)


def window_kernel(
    where_ref, low_ref, high_ref, wet_ref, coef_ref, stations_ref, *refs,
    tile_rows, grid_rows,
):
    cov_refs, (pf_out, sensed_out, state_a, state_b, press, flux, turned) = refs[:-7], refs[-7:]
    first_row = where_ref[0]
    ext = tile_rows + 2 * DEPTH
    groups = len(cov_refs)
    cells = 128 * groups
    stride = 6 * tile_rows
    halves = range(GROUP // 8)

    def at(ref, field, r, kg):
        return [ref[field, r, pl.ds(8 * kg, 8), pl.ds(128 * c, 128)] for c in range(groups)]

    def put(ref, field, r, kg, parts):
        for c in range(groups):
            ref[field, r, pl.ds(8 * kg, 8), pl.ds(128 * c, 128)] = parts[c]

    def spread(ref, index, r):
        rows = ref.shape[0] // groups
        return [ref[pl.ds(c * rows + index * ext + r, 8, stride=0), :] for c in range(groups)]

    size = turned_size(tile_rows)
    for f in range(6):
        for c in range(groups):
            base = (f * groups + c) * size
            turn(cov_refs[c], f * tile_rows, stride, turned, base, tile_rows)
            for r in range(tile_rows):
                state_a[f, DEPTH + r, :, pl.ds(128 * c, 128)] = turned_row(turned, base, r)
    for i, (field, d) in enumerate(halo_rows()):
        state_a[field, DEPTH - d] = low_ref[i].astype(f32)
        state_a[field, DEPTH + tile_rows + d - 1] = high_ref[i].astype(f32)
    for layer in range(2):
        for r in (1, ext - 2):
            state_a[3 * layer + 2, r] = jnp.zeros((GROUP, cells), f32)

    def press_of(top, bottom):
        p_top = gravity * (top + bottom)
        return p_top, p_top - reduced_gravity * top

    def first_press(r, carry):
        press[0, r], press[1, r] = press_of(state_a[0, r], state_a[3, r])
        return carry

    lax.fori_loop(0, ext, first_press, 0, unroll=2)
    lane = lax.broadcasted_iota(jnp.int32, (8, 128), 1)

    def move(t, src, dst, r_first, count, edge=False):
        stores = []
        for r in [r_first + k for k in range(count)]:
            wet_a, wet_b, wet_c = (spread(wet_ref, q, r) for q in range(3))
            for layer in range(2):
                depth, mu, mv = (spread(coef_ref, t * 6 + 3 * layer + q, r) for q in range(3))
                for kg in halves:
                    h = at(src, 3 * layer, r, kg)
                    u = at(src, 3 * layer + 1, r, kg)
                    v = at(src, 3 * layer + 2, r, kg)
                    before = at(press, layer, r - 1, kg)
                    after = at(press, layer, r + 1, kg)
                    if edge:
                        u_new, along = [], []
                        for c in range(groups):
                            u_c = (
                                wet_a[c] * u[c] + wet_b[c] * v[c] - wet_c[c] * (after[c] - before[c])
                            )
                            along.append(depth[c] * u_c + h[c] * mu[c])
                        stores.append((flux, layer, r, kg, along))
                        continue
                    slope = lane_steps(at(press, layer, r, kg), lane)
                    u_new, v_new, along, cross = [], [], [], []
                    for c in range(groups):
                        u_c = wet_a[c] * u[c] + wet_b[c] * v[c] - wet_c[c] * (after[c] - before[c])
                        v_c = wet_a[c] * v[c] - wet_b[c] * u[c] - wet_c[c] * slope[c]
                        u_new.append(u_c)
                        v_new.append(v_c)
                        along.append(depth[c] * u_c + h[c] * mu[c])
                        cross.append(depth[c] * v_c + h[c] * mv[c])
                    cross = lane_steps(cross, lane)
                    part = [h[c] - cross[c] for c in range(groups)]
                    stores += [
                        (dst, 3 * layer, r, kg, part),
                        (dst, 3 * layer + 1, r, kg, u_new),
                        (dst, 3 * layer + 2, r, kg, v_new),
                        (flux, layer, r, kg, along),
                    ]
        for store in stores:
            put(*store)

    def rise(t, dst, r_first, count):
        stores = []
        for r in [r_first + k for k in range(count)]:
            g = first_row - DEPTH + r
            keep = jnp.where(jnp.logical_and(g >= 0, g < grid_rows), 1.0, 0.0).astype(f32)
            for kg in halves:
                fresh = []
                for layer in range(2):
                    part = at(dst, 3 * layer, r, kg)
                    before, after = at(flux, layer, r - 1, kg), at(flux, layer, r + 1, kg)
                    fresh.append(
                        [keep * (part[c] - (after[c] - before[c])) for c in range(groups)]
                    )
                    stores.append((dst, 3 * layer, r, kg, fresh[-1]))
                if t < ITERS - 1:
                    both = [press_of(fresh[0][c], fresh[1][c]) for c in range(groups)]
                    for layer in range(2):
                        stores.append((press, layer, r, kg, [p[layer] for p in both]))
        for store in stores:
            put(*store)

    src, dst = state_a, state_b
    for t in range(ITERS):
        first = 2 * t + 2
        rows = ext - 4 * t - 4
        pace = 4 if rows % 4 == 0 else (2 if rows % 2 == 0 else 1)
        move(t, src, dst, first - 1, 1, edge=True)
        move(t, src, dst, first + rows, 1, edge=True)

        def move_body(i, carry, t=t, src=src, dst=dst, first=first, pace=pace):
            move(t, src, dst, first + pace * i, pace)
            return carry

        lax.fori_loop(0, rows // pace, move_body, 0)

        def rise_body(i, carry, t=t, dst=dst, first=first, pace=pace):
            rise(t, dst, first + pace * i, pace)
            return carry

        lax.fori_loop(0, rows // pace, rise_body, 0)
        src, dst = dst, src

    n_stations = stations_ref.shape[1]
    total = jnp.zeros((3 * GROUP, n_stations), f32)
    for r in range(tile_rows):
        for f in range(6):
            pf_out[f, r] = src[f, DEPTH + r].astype(bf16)
        surface = src[0, DEPTH + r] + src[3, DEPTH + r]
        high = surface.astype(bf16)
        rest = surface - high.astype(f32)
        middle = rest.astype(bf16)
        low = (rest - middle.astype(f32)).astype(bf16)
        pieces = jnp.concatenate([high, middle, low], axis=0)
        hits = station_hits(stations_ref, r, cells).astype(f32).astype(bf16)
        total = total + jnp.dot(pieces, hits, preferred_element_type=f32)
    sensed_out[...] = (
        total[:GROUP] + (total[GROUP : 2 * GROUP] + total[2 * GROUP : 3 * GROUP])
    )


def gram_kernel(where_ref, weight_ref, innov_ref, *refs, columns):
    sensed_refs, out_ref, both, left = refs[:-3], refs[-3], refs[-2], refs[-1]
    index = where_ref[1]
    count = both.shape[0] // columns
    each = len(sensed_refs) // count
    for d in range(count):
        start = pl.multiple_of(lax.rem(index + d, count) * columns, 8)
        for ref in sensed_refs[d * each : (d + 1) * each]:
            size = ref.shape[0]
            both[pl.ds(start, size), :] = ref[...] * weight_ref[...]
            start = pl.multiple_of(start + size, 8)
    left[pl.ds(0, columns), :] = both[pl.ds(pl.multiple_of(index * columns, 8), columns), :]
    left[pl.ds(columns, 8), :] = innov_ref[...]
    out_ref[...] = lax.dot_general(
        left[...],
        both[...],
        (((1,), (1,)), ((), ())),
        precision=lax.Precision.HIGHEST,
        preferred_element_type=f32,
    )


def factor_kernel(where_ref, *refs, columns):
    gram_refs, mix_out, scr = refs[:-2], refs[-2], refs[-1]
    index = where_ref[1]
    count = len(gram_refs)
    total = count * columns
    for d in range(count):
        start = pl.multiple_of(lax.rem(index + d, count) * columns, 8)
        scr[pl.ds(start, columns), :] = gram_refs[d][pl.ds(0, columns), :]
    blocks = total // 8
    lane = lax.broadcasted_iota(jnp.int32, (8, total), 1)
    sub = lax.broadcasted_iota(jnp.int32, (8, total), 0)
    eye = [(lane == sub + 8 * b).astype(f32) for b in range(blocks)]
    m = [scr[pl.ds(8 * b, 8), :] + eye[b] for b in range(blocks)]
    w = list(eye)

    def column(x, j):
        return jnp.broadcast_to(x[:, j : j + 1], (8, total))

    def row(x, i):
        return jnp.broadcast_to(x[i : i + 1, :], (8, total))

    scaled = []
    for b in range(blocks):
        heads = [column(m[b], 8 * b + i) for i in range(8)]
        z_m, z_w, low = m[b], w[b], w[b]
        pivots = jnp.ones((8, total), f32)
        for i in range(8):
            pivot = row(heads[i], i)
            pivots = jnp.where(sub == i, pivot, pivots)
            inverse = 1.0 / pivot
            here = sub == i
            head = heads[i]
            for k in range(i + 1, 8):
                factor = row(heads[k], i) * inverse
                heads[k] = jnp.where(here, factor, heads[k] - head * factor)
            row_m = row(z_m, i) * inverse
            row_w = row(z_w, i) * inverse
            z_m = jnp.where(here, row_m, z_m - head * row_m)
            z_w = jnp.where(here, row_w, z_w - head * row_w)
            low = jnp.where(sub > i, low - head * row_w, low)
        scaled.append(low / jnp.sqrt(pivots))
        rows_m = [row(z_m, i) for i in range(8)]
        rows_w = [row(z_w, i) for i in range(8)]
        for q in range(b + 1, blocks):
            tails = [column(m[q], 8 * b + i) for i in range(8)]
            m[q] = m[q] - tree_sum([tails[i] * rows_m[i] for i in range(8)])
            w[q] = w[q] - tree_sum([tails[i] * rows_w[i] for i in range(8)])
    target = gram_refs[0][pl.ds(columns, 1), :]
    weights = jnp.zeros((8, total), f32)
    for b in range(blocks):
        scr[pl.ds(8 * b, 8), :] = scaled[b]
        half = jnp.sum(scaled[b] * target, axis=1, keepdims=True)
        weights = weights + scaled[b] * half
    weights = jnp.sum(weights, axis=0, keepdims=True)
    shift = lax.rem(total - index * columns, total)
    mine = scr[pl.ds(pl.multiple_of(index * columns, 8), columns), :]
    mix_out[pl.ds(0, columns), :] = pltpu.roll(mine, shift, 1).astype(bf16)
    weights = pltpu.roll(jnp.broadcast_to(weights, (8, total)), shift, 1)
    high = weights.astype(bf16)
    low = (weights - high.astype(f32)).astype(bf16)
    pad = jnp.zeros((8, total), f32)
    rows = jnp.where(sub == 0, high.astype(f32), jnp.where(sub == 1, low.astype(f32), 0.0))
    mix_out[pl.ds(columns, 16), :] = jnp.concatenate([rows, pad], axis=0).astype(bf16)


def tree_sum(values):
    while len(values) > 1:
        values = [values[i] + values[i + 1] for i in range(0, len(values), 2)]
    return values[0]


def mix_kernel(where_ref, mix_ref, mean_ref, *refs, columns):
    piece_refs, (cov_out, mean_out, scr, turned) = refs[:-4], refs[-4:]
    tile_rows, cells = mean_ref.shape[1:]
    groups = cells // 128
    piece = mean_out.shape[2]
    mix = mix_ref[...]
    pitch = tile_rows + 1
    for r in range(tile_rows):
        stack = jnp.concatenate([ref[0, r] for ref in piece_refs], axis=0)
        result = jnp.dot(mix, stack, preferred_element_type=f32)
        for c in range(groups):
            for j in range(0, columns, 8):
                turned[c, pl.ds(j * pitch + r, 8, stride=pitch), :] = result[
                    j : j + 8, 128 * c : 128 * c + 128
                ]
        scr[pl.ds(r, 1), :] = result[columns : columns + 1] + result[columns + 1 : columns + 2]
    for j in range(columns):
        for c in range(groups):
            for r in range(0, tile_rows, 8):
                cov_out[j, 0, pl.ds(r, 8), pl.ds(128 * c, 128)] = turned[
                    c, pl.ds(j * pitch + r, 8, stride=1), :
                ]
    whole = mean_ref[0] + scr[...]
    shift = lax.rem(cells - where_ref[1] * piece, cells)
    mean_out[0] = pltpu.roll(whole, shift, 1)[:, :piece]


def spread_sum(value, axis):
    count = lax.axis_size(axis)
    if count & (count - 1):
        return lax.psum(value, axis)
    step = 1
    while step < count:
        value = value + lax.ppermute(value, axis, [(i, i ^ step) for i in range(count)])
        step *= 2
    return value


def shifted(value, axis):
    count = lax.axis_size(axis)
    return [value] + [
        lax.ppermute(value, axis, [((i + d) % count, i) for i in range(count)])
        for d in range(1, count)
    ]


def grant(mib):
    return pltpu.CompilerParams(vmem_limit_bytes=mib << 20)


def in_hbm(value):
    return pltpu.with_memory_space_constraint(value, pltpu.HBM)


def whole_spec(shape):
    return pl.BlockSpec(shape, lambda *_: (0,) * len(shape))


def chunk_list(count):
    if count < 3:
        return [(g, 1) for g in range(count)]
    return [(0, 1), (1, count - 2), (count - 1, 1)]


def local(mean_state, covariance, land_mask, stations, observed, obs_weight):
    columns, _, tile_rows, cells = covariance.shape
    piece = mean_state.shape[2]
    n_space = lax.axis_size("space")
    n_cols = lax.axis_size("cols")
    total = columns * n_cols
    grid_rows = tile_rows * n_space
    ext = tile_rows + 2 * DEPTH
    n_stations = stations.shape[0]
    chunks = chunk_list(columns // GROUP)
    n_halo = len(halo_rows())
    groups = cells // 128
    space_index = lax.axis_index("space")
    column_index = lax.axis_index("cols")
    first_row = space_index * tile_rows
    where = jnp.stack([first_row, column_index]).astype(jnp.int32)
    up = [(i, i + 1) for i in range(n_space - 1)]
    down = [(i + 1, i) for i in range(n_space - 1)]
    smem = pl.BlockSpec(memory_space=pltpu.SMEM)

    flat = covariance.reshape(columns * 6 * tile_rows, cells)
    span = GROUP * 6 * tile_rows


    def cov_specs(start):
        return [pl.BlockSpec((span, 128), lambda i, g=g: (start + i, g)) for g in range(groups)]

    halo_spec = pl.BlockSpec((n_halo, GROUP, cells), lambda i: (0, i, 0))
    lows, highs = [], []
    source = flat
    for c, (start, size) in enumerate(chunks):
        rows = n_halo + 3 if c == 0 else n_halo
        halo_shape = jax.ShapeDtypeStruct((rows, size * GROUP, cells), bf16)
        halo_out = pl.BlockSpec((rows, GROUP, cells), lambda i: (0, i, 0))
        going_up, going_down = pl.pallas_call(
            functools.partial(pack_kernel, tile_rows=tile_rows, with_mean=c == 0),
            grid=(size,),
            in_specs=[whole_spec(mean_state.shape)] * (c == 0) + cov_specs(start),
            out_specs=[halo_out] * 2,
            out_shape=[halo_shape, halo_shape],
            scratch_shapes=[pltpu.VMEM((6 * groups * turned_size(tile_rows), 128), f32)],
            compiler_params=grant(9),
        )(*[in_hbm(mean_state)] * (c == 0), *[in_hbm(source)] * groups)
        source, going_up, going_down = lax.optimization_barrier((flat, going_up, going_down))
        lows.append(lax.ppermute(going_up, "space", up))
        highs.append(lax.ppermute(going_down, "space", down))


    def mean_halo(payload):
        parts = payload[n_halo:].astype(f32)
        value = parts[:, :, :piece] + parts[:, :, 128 : 128 + piece]
        return value.reshape(6, DEPTH, piece)

    mean_ext = jnp.concatenate([mean_halo(lows[0]), mean_state, mean_halo(highs[0])], axis=1)
    mean_ext = lax.all_gather(mean_ext, "cols", axis=2, tiled=True)
    station_row = (stations - first_row * cells).astype(jnp.int32)[None, :]
    weight_row = obs_weight[None, :]
    mean_run = pl.pallas_call(
        functools.partial(mean_kernel, tile_rows=tile_rows, grid_rows=grid_rows),
        in_specs=[smem] + [pl.BlockSpec(memory_space=pltpu.VMEM)] * 5,
        out_specs=[pl.BlockSpec(memory_space=pltpu.VMEM)] * 4,
        out_shape=[
            jax.ShapeDtypeStruct((groups * 3 * ext, 128), f32),
            jax.ShapeDtypeStruct((groups * ITERS * 6 * ext, 128), f32),
            jax.ShapeDtypeStruct((6, tile_rows, cells), f32),
            jax.ShapeDtypeStruct((8, n_stations), f32),
        ],
        name="mean_window",
        compiler_params=grant(4),
    )
    wet, coef, mean_final, innovation = mean_run(
        where, mean_ext, land_mask, station_row, observed[None, :], weight_row
    )

    forecasts, sensed = [], []
    for c, (start, size) in enumerate(chunks):
        window = pl.pallas_call(
            functools.partial(window_kernel, tile_rows=tile_rows, grid_rows=grid_rows),
            grid=(size,),
            in_specs=[
                smem,
                halo_spec,
                halo_spec,
                whole_spec((groups * 3 * ext, 128)),
                whole_spec((groups * ITERS * 6 * ext, 128)),
                whole_spec((1, n_stations)),
            ]
            + cov_specs(start),
            out_specs=[
                pl.BlockSpec((6, tile_rows, GROUP, cells), lambda i: (0, 0, i, 0)),
                pl.BlockSpec((GROUP, n_stations), lambda i: (i, 0)),
            ],
            out_shape=[
                jax.ShapeDtypeStruct((6, tile_rows, size * GROUP, cells), bf16),
                jax.ShapeDtypeStruct((size * GROUP, n_stations), f32),
            ],
            scratch_shapes=[pltpu.VMEM((n, ext, GROUP, cells), f32) for n in (6, 6, 2, 2)]
            + [pltpu.VMEM((6 * groups * turned_size(tile_rows), 128), f32)],
            compiler_params=grant(22),
        )
        pf, s = window(where, lows[c], highs[c], wet, coef, station_row, *[flat] * groups)
        forecasts.append(shifted(pf, "cols"))
        sensed.append(shifted(s, "cols"))

    sensed_all = [sensed[c][d] for d in range(n_cols) for c in range(len(chunks))]
    gram = pl.pallas_call(
        functools.partial(gram_kernel, columns=columns),
        in_specs=[smem] + [pl.BlockSpec(memory_space=pltpu.VMEM)] * (2 + len(sensed_all)),
        out_specs=pl.BlockSpec(memory_space=pltpu.VMEM),
        out_shape=jax.ShapeDtypeStruct((columns + 8, total), f32),
        scratch_shapes=[
            pltpu.VMEM((total, n_stations), f32),
            pltpu.VMEM((columns + 8, n_stations), f32),
        ],
        name="gram",
        compiler_params=grant(2),
    )(where, weight_row, innovation, *sensed_all)
    gram_all = shifted(spread_sum(gram, "space"), "cols")
    mix = pl.pallas_call(
        functools.partial(factor_kernel, columns=columns),
        in_specs=[smem] + [pl.BlockSpec(memory_space=pltpu.VMEM)] * n_cols,
        out_specs=pl.BlockSpec(memory_space=pltpu.VMEM),
        out_shape=jax.ShapeDtypeStruct((columns + 16, total), bf16),
        scratch_shapes=[pltpu.VMEM((total, total), f32)],
        name="factor",
        compiler_params=grant(2),
    )(where, *gram_all)

    pieces = [forecasts[c][d] for d in range(n_cols) for c in range(len(chunks))]
    updated, mean_out = pl.pallas_call(
        functools.partial(mix_kernel, columns=columns),
        grid=(6,),
        in_specs=[
            smem,
            whole_spec((columns + 16, total)),
            pl.BlockSpec((1, tile_rows, cells), lambda f: (f, 0, 0)),
        ]
        + [
            pl.BlockSpec((1, tile_rows, p.shape[2], cells), lambda f: (f, 0, 0, 0)) for p in pieces
        ],
        out_specs=[
            pl.BlockSpec((columns, 1, tile_rows, cells), lambda f: (0, f, 0, 0)),
            pl.BlockSpec((1, tile_rows, piece), lambda f: (f, 0, 0)),
        ],
        out_shape=[
            jax.ShapeDtypeStruct((columns, 6, tile_rows, cells), f32),
            jax.ShapeDtypeStruct((6, tile_rows, piece), f32),
        ],
        scratch_shapes=[
            pltpu.VMEM((tile_rows, cells), f32),
            pltpu.VMEM((groups, columns * (tile_rows + 1) + 8, 128), f32),
        ],
        name="mix",
        compiler_params=grant(10),
    )(where, mix, mean_final, *pieces)
    return (mean_out, updated)


def solution(mesh):
    return jax.shard_map(
        local,
        mesh=mesh,
        in_specs=(
            P(None, "space", "cols"),
            P("cols", None, "space", None),
            P(),
            P("space"),
            P("space"),
            P("space"),
        ),
        out_specs=(P(None, "space", "cols"), P("cols", None, "space", None)),
        check_vma=False,
    )
```

```python
import functools

import jax
import jax.numpy as jnp
from jax import lax
from jax.experimental import pallas as pl
from jax.experimental.pallas import tpu as pltpu
from jax.sharding import PartitionSpec as P


ITERS = 4
DEPTH = 2 * ITERS
GROUP = 16

time_step = 0.5
gravity = 1.0
reduced_gravity = 0.125
coriolis = 0.3
friction = 0.05
layer_depths = (1.0, 2.0)

keep_part = 1.0 - time_step * friction
turn_part = time_step * coriolis
slope_part = 0.5 * time_step

f32 = jnp.float32
bf16 = jnp.bfloat16


def halo_rows():
    rows = []
    for layer in range(2):
        rows += [(3 * layer, d) for d in range(DEPTH - 1, 0, -1)]
    for layer in range(2):
        rows += [(3 * layer + 1, d) for d in range(DEPTH - 1, 0, -1)]
        rows += [(3 * layer + 2, d) for d in range(DEPTH - 2, 0, -1)]
    return rows


def turn(src_ref, src_row, stride, turned, base, tile_rows):
    pitch = GROUP + 1
    for k in range(GROUP):
        for r in range(0, tile_rows, 8):
            turned[pl.ds(base + r * pitch + k, 8, stride=pitch), :] = src_ref[
                pl.ds(k * stride + src_row + r, 8), :
            ]


def turned_row(turned, base, r):
    pitch = GROUP + 1
    return jnp.concatenate(
        [turned[pl.ds(base + r * pitch + 8 * kg, 8, stride=1), :] for kg in range(GROUP // 8)],
        axis=0,
    )


def turned_size(tile_rows):
    return tile_rows * (GROUP + 1) + 8


def pack_kernel(*refs, tile_rows, with_mean):
    cov_refs, (up_ref, down_ref, turned) = refs[:-3], refs[-3:]
    if with_mean:
        mean_ref, cov_refs = cov_refs[0], cov_refs[1:]
        piece = mean_ref.shape[2]
        for i in range(3):
            for ref, r in ((up_ref, tile_rows - DEPTH), (down_ref, 0)):
                value = jnp.concatenate(
                    [mean_ref[f, pl.ds(r, DEPTH), :] for f in (2 * i, 2 * i + 1)], axis=0
                )
                high = value.astype(bf16)
                low = (value - high.astype(f32)).astype(bf16)
                ref[len(halo_rows()) + i, :, pl.ds(0, piece)] = high
                ref[len(halo_rows()) + i, :, pl.ds(128, piece)] = low
    stride = 6 * tile_rows
    size = turned_size(tile_rows)
    groups = len(cov_refs)
    for f in range(6):
        for c in range(groups):
            turn(cov_refs[c], f * tile_rows, stride, turned, (f * groups + c) * size, tile_rows)

    def row(field, r):
        return jnp.concatenate(
            [turned_row(turned, (field * groups + c) * size, r) for c in range(groups)], axis=1
        )

    for i, (field, d) in enumerate(halo_rows()):
        for ref, r, side in ((up_ref, tile_rows - d, -1), (down_ref, d - 1, 1)):
            value = row(field, r)
            if d == DEPTH - 1 and field % 3 == 1:
                top = row(0, r + side)
                beyond = gravity * (top + row(3, r + side))
                if field > 3:
                    beyond = beyond - reduced_gravity * top
                value = value + (turn_part / keep_part) * row(field + 1, r)
                value = value - (side * slope_part / keep_part) * beyond
            ref[i] = value.astype(bf16)


def lane_steps(parts, lane):
    n = len(parts)
    right = [pltpu.roll(p, 1, 1) for p in parts]
    left = [pltpu.roll(p, 127, 1) for p in parts]
    out = []
    for i in range(n):
        before = jnp.where(lane == 0, right[i - 1] if i > 0 else 0.0, right[i])
        after = jnp.where(lane == 127, left[i + 1] if i < n - 1 else 0.0, left[i])
        out.append(after - before)
    return out


def station_hits(stations_ref, r, cells):
    position = lax.broadcasted_iota(jnp.int32, (cells, stations_ref.shape[1]), 0) + r * cells
    return position == stations_ref[...]


def mean_kernel(
    where_ref, mean_ref, mask_ref, stations_ref, observed_ref, weight_ref,
    wet_out, coef_out, final_out, innov_out, *, tile_rows, grid_rows,
):
    first_row = where_ref[0]
    ext, cells = mean_ref.shape[1:]
    wets = []
    for i in range(ext // 8):
        g = first_row - DEPTH + 8 * i
        inside = jnp.logical_and(g >= 0, g < grid_rows).astype(f32)
        start = pl.multiple_of(jnp.clip(g, 0, grid_rows - 8), 8)
        wets.append(mask_ref[pl.ds(start, 8), :].astype(f32) * inside)
    wet = jnp.concatenate(wets, axis=0)
    g_all = first_row - DEPTH + lax.broadcasted_iota(jnp.int32, (ext, cells), 0)
    keep = jnp.logical_and(g_all >= 0, g_all < grid_rows).astype(f32)
    lane_all = lax.broadcasted_iota(jnp.int32, (ext, cells), 1)

    def put(ref, index, value):
        rows = ref.shape[0] // (cells // 128)
        for c in range(cells // 128):
            ref[pl.ds(c * rows + index * ext, ext), :] = value[:, 128 * c : 128 * c + 128]

    put(wet_out, 0, wet * keep_part)
    put(wet_out, 1, wet * turn_part)
    put(wet_out, 2, wet * slope_part)

    def diff_rows(a):
        return 0.5 * (pltpu.roll(a, ext - 1, 0) - pltpu.roll(a, 1, 0))

    def diff_cols(a):
        after = jnp.where(lane_all == cells - 1, 0.0, pltpu.roll(a, cells - 1, 1))
        before = jnp.where(lane_all == 0, 0.0, pltpu.roll(a, 1, 1))
        return 0.5 * (after - before)

    state = [mean_ref[f] for f in range(6)]
    for t in range(ITERS):
        pressure_top = gravity * (state[0] + state[3])
        pressures = (pressure_top, pressure_top - reduced_gravity * state[0])
        fresh = []
        for layer in range(2):
            h, u, v = state[3 * layer : 3 * layer + 3]
            p = pressures[layer]
            u_new = wet * (u + time_step * (-diff_rows(p) + coriolis * v - friction * u))
            v_new = wet * (v + time_step * (-diff_cols(p) - coriolis * u - friction * v))
            depth = layer_depths[layer] + h
            h_new = h - time_step * (diff_rows(depth * u_new) + diff_cols(depth * v_new))
            for q, value in enumerate((depth, u_new, v_new)):
                put(coef_out, t * 6 + 3 * layer + q, slope_part * value)
            fresh += [h_new * keep, u_new, v_new]
        state = fresh
    for f in range(6):
        final_out[f] = state[f][DEPTH : DEPTH + tile_rows, :]
    surface = (state[0] + state[3])[DEPTH : DEPTH + tile_rows, :]
    n_stations = stations_ref.shape[1]
    sublane = lax.broadcasted_iota(jnp.int32, (8, n_stations), 0)
    picked = jnp.zeros((8, n_stations), f32)
    for r in range(tile_rows):
        hits = station_hits(stations_ref, r, cells).astype(f32)
        block = surface[r // 8 * 8 : r // 8 * 8 + 8, :]
        values = jnp.dot(block, hits, precision=lax.Precision.HIGHEST, preferred_element_type=f32)
        picked = picked + jnp.where(sublane == r % 8, values, 0.0)
    at_station = jnp.sum(picked, axis=0, keepdims=True)
    innovation = weight_ref[...] * (observed_ref[...] - at_station)
    innov_out[...] = jnp.where(sublane == 0, innovation, 0.0)


def window_kernel(
    where_ref, low_ref, high_ref, wet_ref, coef_ref, stations_ref, *refs,
    tile_rows, grid_rows,
):
    cov_refs, (pf_out, sensed_out, state_a, state_b, press, flux, turned) = refs[:-7], refs[-7:]
    first_row = where_ref[0]
    ext = tile_rows + 2 * DEPTH
    groups = len(cov_refs)
    cells = 128 * groups
    stride = 6 * tile_rows
    halves = range(GROUP // 8)

    def at(ref, field, r, kg):
        return [ref[field, r, pl.ds(8 * kg, 8), pl.ds(128 * c, 128)] for c in range(groups)]

    def put(ref, field, r, kg, parts):
        for c in range(groups):
            ref[field, r, pl.ds(8 * kg, 8), pl.ds(128 * c, 128)] = parts[c]

    def spread(ref, index, r):
        rows = ref.shape[0] // groups
        return [ref[pl.ds(c * rows + index * ext + r, 8, stride=0), :] for c in range(groups)]

    size = turned_size(tile_rows)
    for f in range(6):
        for c in range(groups):
            base = (f * groups + c) * size
            turn(cov_refs[c], f * tile_rows, stride, turned, base, tile_rows)
            for r in range(tile_rows):
                state_a[f, DEPTH + r, :, pl.ds(128 * c, 128)] = turned_row(turned, base, r)
    for i, (field, d) in enumerate(halo_rows()):
        state_a[field, DEPTH - d] = low_ref[i].astype(f32)
        state_a[field, DEPTH + tile_rows + d - 1] = high_ref[i].astype(f32)
    for layer in range(2):
        for r in (1, ext - 2):
            state_a[3 * layer + 2, r] = jnp.zeros((GROUP, cells), f32)
        for r in (0, ext - 1):
            state_a[3 * layer, r] = jnp.zeros((GROUP, cells), f32)

    def press_of(top, bottom):
        p_top = gravity * (top + bottom)
        return p_top, p_top - reduced_gravity * top

    def first_press(r, carry):
        press[0, r], press[1, r] = press_of(state_a[0, r], state_a[3, r])
        return carry

    lax.fori_loop(0, ext, first_press, 0, unroll=2)
    lane = lax.broadcasted_iota(jnp.int32, (8, 128), 1)

    def move(t, src, dst, r_first, count, edge=False):
        stores = []
        for r in [r_first + k for k in range(count)]:
            wet_a, wet_b, wet_c = (spread(wet_ref, q, r) for q in range(3))
            for layer in range(2):
                depth, mu, mv = (spread(coef_ref, t * 6 + 3 * layer + q, r) for q in range(3))
                for kg in halves:
                    h = at(src, 3 * layer, r, kg)
                    u = at(src, 3 * layer + 1, r, kg)
                    v = at(src, 3 * layer + 2, r, kg)
                    before = at(press, layer, r - 1, kg)
                    after = at(press, layer, r + 1, kg)
                    if edge:
                        u_new, along = [], []
                        for c in range(groups):
                            u_c = (
                                wet_a[c] * u[c] + wet_b[c] * v[c] - wet_c[c] * (after[c] - before[c])
                            )
                            along.append(depth[c] * u_c + h[c] * mu[c])
                        stores.append((flux, layer, r, kg, along))
                        continue
                    slope = lane_steps(at(press, layer, r, kg), lane)
                    u_new, v_new, along, cross = [], [], [], []
                    for c in range(groups):
                        u_c = wet_a[c] * u[c] + wet_b[c] * v[c] - wet_c[c] * (after[c] - before[c])
                        v_c = wet_a[c] * v[c] - wet_b[c] * u[c] - wet_c[c] * slope[c]
                        u_new.append(u_c)
                        v_new.append(v_c)
                        along.append(depth[c] * u_c + h[c] * mu[c])
                        cross.append(depth[c] * v_c + h[c] * mv[c])
                    cross = lane_steps(cross, lane)
                    part = [h[c] - cross[c] for c in range(groups)]
                    stores += [
                        (dst, 3 * layer, r, kg, part),
                        (dst, 3 * layer + 1, r, kg, u_new),
                        (dst, 3 * layer + 2, r, kg, v_new),
                        (flux, layer, r, kg, along),
                    ]
        for store in stores:
            put(*store)

    def rise(t, dst, r_first, count):
        stores = []
        for r in [r_first + k for k in range(count)]:
            g = first_row - DEPTH + r
            keep = jnp.where(jnp.logical_and(g >= 0, g < grid_rows), 1.0, 0.0).astype(f32)
            for kg in halves:
                fresh = []
                for layer in range(2):
                    part = at(dst, 3 * layer, r, kg)
                    before, after = at(flux, layer, r - 1, kg), at(flux, layer, r + 1, kg)
                    fresh.append(
                        [keep * (part[c] - (after[c] - before[c])) for c in range(groups)]
                    )
                    stores.append((dst, 3 * layer, r, kg, fresh[-1]))
                if t < ITERS - 1:
                    both = [press_of(fresh[0][c], fresh[1][c]) for c in range(groups)]
                    for layer in range(2):
                        stores.append((press, layer, r, kg, [p[layer] for p in both]))
        for store in stores:
            put(*store)

    src, dst = state_a, state_b
    for t in range(ITERS):
        first = 2 * t + 2
        rows = ext - 4 * t - 4
        pace = 4 if rows % 4 == 0 else (2 if rows % 2 == 0 else 1)
        move(t, src, dst, first - 1, 1, edge=True)
        move(t, src, dst, first + rows, 1, edge=True)

        def move_body(i, carry, t=t, src=src, dst=dst, first=first, pace=pace):
            move(t, src, dst, first + pace * i, pace)
            return carry

        lax.fori_loop(0, rows // pace, move_body, 0)

        def rise_body(i, carry, t=t, dst=dst, first=first, pace=pace):
            rise(t, dst, first + pace * i, pace)
            return carry

        lax.fori_loop(0, rows // pace, rise_body, 0)
        src, dst = dst, src

    n_stations = stations_ref.shape[1]
    total = jnp.zeros((3 * GROUP, n_stations), f32)
    for r in range(tile_rows):
        for f in range(6):
            pf_out[f, r] = src[f, DEPTH + r].astype(bf16)
        surface = src[0, DEPTH + r] + src[3, DEPTH + r]
        high = surface.astype(bf16)
        rest = surface - high.astype(f32)
        middle = rest.astype(bf16)
        low = (rest - middle.astype(f32)).astype(bf16)
        pieces = jnp.concatenate([high, middle, low], axis=0)
        hits = station_hits(stations_ref, r, cells).astype(f32).astype(bf16)
        total = total + jnp.dot(pieces, hits, preferred_element_type=f32)
    sensed_out[...] = (
        total[:GROUP] + (total[GROUP : 2 * GROUP] + total[2 * GROUP : 3 * GROUP])
    )


def gram_kernel(where_ref, weight_ref, innov_ref, *refs, columns):
    sensed_refs, out_ref, both, left = refs[:-3], refs[-3], refs[-2], refs[-1]
    index = where_ref[1]
    count = both.shape[0] // columns
    each = len(sensed_refs) // count
    for d in range(count):
        start = pl.multiple_of(lax.rem(index + d, count) * columns, 8)
        for ref in sensed_refs[d * each : (d + 1) * each]:
            size = ref.shape[0]
            both[pl.ds(start, size), :] = ref[...] * weight_ref[...]
            start = pl.multiple_of(start + size, 8)
    left[pl.ds(0, columns), :] = both[pl.ds(pl.multiple_of(index * columns, 8), columns), :]
    left[pl.ds(columns, 8), :] = innov_ref[...]
    out_ref[...] = lax.dot_general(
        left[...],
        both[...],
        (((1,), (1,)), ((), ())),
        precision=lax.Precision.HIGHEST,
        preferred_element_type=f32,
    )


def factor_kernel(where_ref, *refs, columns):
    gram_refs, mix_out, scr = refs[:-2], refs[-2], refs[-1]
    index = where_ref[1]
    count = len(gram_refs)
    total = count * columns
    for d in range(count):
        start = pl.multiple_of(lax.rem(index + d, count) * columns, 8)
        scr[pl.ds(start, columns), :] = gram_refs[d][pl.ds(0, columns), :]
    blocks = total // 8
    lane = lax.broadcasted_iota(jnp.int32, (8, total), 1)
    sub = lax.broadcasted_iota(jnp.int32, (8, total), 0)
    eye = [(lane == sub + 8 * b).astype(f32) for b in range(blocks)]
    m = [scr[pl.ds(8 * b, 8), :] + eye[b] for b in range(blocks)]
    w = list(eye)

    def column(x, j):
        return jnp.broadcast_to(x[:, j : j + 1], (8, total))

    def row(x, i):
        return jnp.broadcast_to(x[i : i + 1, :], (8, total))

    scaled = []
    for b in range(blocks):
        heads = [column(m[b], 8 * b + i) for i in range(8)]
        z_m, z_w, low = m[b], w[b], w[b]
        pivots = jnp.ones((8, total), f32)
        for i in range(8):
            pivot = row(heads[i], i)
            pivots = jnp.where(sub == i, pivot, pivots)
            inverse = 1.0 / pivot
            here = sub == i
            head = heads[i]
            for k in range(i + 1, 8):
                factor = row(heads[k], i) * inverse
                heads[k] = jnp.where(here, factor, heads[k] - head * factor)
            row_m = row(z_m, i) * inverse
            row_w = row(z_w, i) * inverse
            z_m = jnp.where(here, row_m, z_m - head * row_m)
            z_w = jnp.where(here, row_w, z_w - head * row_w)
            low = jnp.where(sub > i, low - head * row_w, low)
        scaled.append(low / jnp.sqrt(pivots))
        rows_m = [row(z_m, i) for i in range(8)]
        rows_w = [row(z_w, i) for i in range(8)]
        for q in range(b + 1, blocks):
            tails = [column(m[q], 8 * b + i) for i in range(8)]
            m[q] = m[q] - tree_sum([tails[i] * rows_m[i] for i in range(8)])
            w[q] = w[q] - tree_sum([tails[i] * rows_w[i] for i in range(8)])
    target = gram_refs[0][pl.ds(columns, 1), :]
    weights = jnp.zeros((8, total), f32)
    for b in range(blocks):
        scr[pl.ds(8 * b, 8), :] = scaled[b]
        half = jnp.sum(scaled[b] * target, axis=1, keepdims=True)
        weights = weights + scaled[b] * half
    weights = jnp.sum(weights, axis=0, keepdims=True)
    shift = lax.rem(total - index * columns, total)
    mine = scr[pl.ds(pl.multiple_of(index * columns, 8), columns), :]
    mix_out[pl.ds(0, columns), :] = pltpu.roll(mine, shift, 1).astype(bf16)
    weights = pltpu.roll(jnp.broadcast_to(weights, (8, total)), shift, 1)
    high = weights.astype(bf16)
    low = (weights - high.astype(f32)).astype(bf16)
    pad = jnp.zeros((8, total), f32)
    rows = jnp.where(sub == 0, high.astype(f32), jnp.where(sub == 1, low.astype(f32), 0.0))
    mix_out[pl.ds(columns, 16), :] = jnp.concatenate([rows, pad], axis=0).astype(bf16)


def tree_sum(values):
    while len(values) > 1:
        values = [values[i] + values[i + 1] for i in range(0, len(values), 2)]
    return values[0]


def mix_kernel(where_ref, mix_ref, mean_ref, *refs, columns):
    piece_refs, (cov_out, mean_out, scr, turned) = refs[:-4], refs[-4:]
    tile_rows, cells = mean_ref.shape[1:]
    groups = cells // 128
    piece = mean_out.shape[2]
    mix = mix_ref[...]
    pitch = tile_rows + 1
    for r in range(tile_rows):
        stack = jnp.concatenate([ref[0, r] for ref in piece_refs], axis=0)
        result = jnp.dot(mix, stack, preferred_element_type=f32)
        for c in range(groups):
            for j in range(0, columns, 8):
                turned[c, pl.ds(j * pitch + r, 8, stride=pitch), :] = result[
                    j : j + 8, 128 * c : 128 * c + 128
                ]
        scr[pl.ds(r, 1), :] = result[columns : columns + 1] + result[columns + 1 : columns + 2]
    for j in range(columns):
        for c in range(groups):
            for r in range(0, tile_rows, 8):
                cov_out[j, 0, pl.ds(r, 8), pl.ds(128 * c, 128)] = turned[
                    c, pl.ds(j * pitch + r, 8, stride=1), :
                ]
    whole = mean_ref[0] + scr[...]
    shift = lax.rem(cells - where_ref[1] * piece, cells)
    mean_out[0] = pltpu.roll(whole, shift, 1)[:, :piece]


def spread_sum(value, axis):
    count = lax.axis_size(axis)
    if count & (count - 1):
        return lax.psum(value, axis)
    step = 1
    while step < count:
        value = value + lax.ppermute(value, axis, [(i, i ^ step) for i in range(count)])
        step *= 2
    return value


def shifted(value, axis):
    count = lax.axis_size(axis)
    return [value] + [
        lax.ppermute(value, axis, [((i + d) % count, i) for i in range(count)])
        for d in range(1, count)
    ]


def grant(mib):
    return pltpu.CompilerParams(vmem_limit_bytes=mib << 20)


def in_hbm(value):
    return pltpu.with_memory_space_constraint(value, pltpu.HBM)


def whole_spec(shape):
    return pl.BlockSpec(shape, lambda *_: (0,) * len(shape))


def chunk_list(count):
    if count < 3:
        return [(g, 1) for g in range(count)]
    return [(0, 1), (1, count - 2), (count - 1, 1)]


def local(mean_state, covariance, land_mask, stations, observed, obs_weight):
    columns, _, tile_rows, cells = covariance.shape
    piece = mean_state.shape[2]
    n_space = lax.axis_size("space")
    n_cols = lax.axis_size("cols")
    total = columns * n_cols
    grid_rows = tile_rows * n_space
    ext = tile_rows + 2 * DEPTH
    n_stations = stations.shape[0]
    chunks = chunk_list(columns // GROUP)
    n_halo = len(halo_rows())
    groups = cells // 128
    space_index = lax.axis_index("space")
    column_index = lax.axis_index("cols")
    first_row = space_index * tile_rows
    where = jnp.stack([first_row, column_index]).astype(jnp.int32)
    up = [(i, i + 1) for i in range(n_space - 1)]
    down = [(i + 1, i) for i in range(n_space - 1)]
    smem = pl.BlockSpec(memory_space=pltpu.SMEM)

    flat = covariance.reshape(columns * 6 * tile_rows, cells)
    span = GROUP * 6 * tile_rows


    def cov_specs(start):
        return [pl.BlockSpec((span, 128), lambda i, g=g: (start + i, g)) for g in range(groups)]

    halo_spec = pl.BlockSpec((n_halo, GROUP, cells), lambda i: (0, i, 0))
    lows, highs = [], []
    source = flat
    for c, (start, size) in enumerate(chunks):
        rows = n_halo + 3 if c == 0 else n_halo
        halo_shape = jax.ShapeDtypeStruct((rows, size * GROUP, cells), bf16)
        halo_out = pl.BlockSpec((rows, GROUP, cells), lambda i: (0, i, 0))
        going_up, going_down = pl.pallas_call(
            functools.partial(pack_kernel, tile_rows=tile_rows, with_mean=c == 0),
            grid=(size,),
            in_specs=[whole_spec(mean_state.shape)] * (c == 0) + cov_specs(start),
            out_specs=[halo_out] * 2,
            out_shape=[halo_shape, halo_shape],
            scratch_shapes=[pltpu.VMEM((6 * groups * turned_size(tile_rows), 128), f32)],
            compiler_params=grant(9),
        )(*[in_hbm(mean_state)] * (c == 0), *[in_hbm(source)] * groups)
        source, going_up, going_down = lax.optimization_barrier((flat, going_up, going_down))
        lows.append(lax.ppermute(going_up, "space", up))
        highs.append(lax.ppermute(going_down, "space", down))


    def mean_halo(payload):
        parts = payload[n_halo:].astype(f32)
        value = parts[:, :, :piece] + parts[:, :, 128 : 128 + piece]
        return value.reshape(6, DEPTH, piece)

    mean_ext = jnp.concatenate([mean_halo(lows[0]), mean_state, mean_halo(highs[0])], axis=1)
    mean_ext = lax.all_gather(mean_ext, "cols", axis=2, tiled=True)
    station_row = (stations - first_row * cells).astype(jnp.int32)[None, :]
    weight_row = obs_weight[None, :]
    mean_run = pl.pallas_call(
        functools.partial(mean_kernel, tile_rows=tile_rows, grid_rows=grid_rows),
        in_specs=[smem] + [pl.BlockSpec(memory_space=pltpu.VMEM)] * 5,
        out_specs=[pl.BlockSpec(memory_space=pltpu.VMEM)] * 4,
        out_shape=[
            jax.ShapeDtypeStruct((groups * 3 * ext, 128), f32),
            jax.ShapeDtypeStruct((groups * ITERS * 6 * ext, 128), f32),
            jax.ShapeDtypeStruct((6, tile_rows, cells), f32),
            jax.ShapeDtypeStruct((8, n_stations), f32),
        ],
        name="mean_window",
        compiler_params=grant(4),
    )
    wet, coef, mean_final, innovation = mean_run(
        where, mean_ext, land_mask, station_row, observed[None, :], weight_row
    )

    forecasts, sensed = [], []
    for c, (start, size) in enumerate(chunks):
        window = pl.pallas_call(
            functools.partial(window_kernel, tile_rows=tile_rows, grid_rows=grid_rows),
            grid=(size,),
            in_specs=[
                smem,
                halo_spec,
                halo_spec,
                whole_spec((groups * 3 * ext, 128)),
                whole_spec((groups * ITERS * 6 * ext, 128)),
                whole_spec((1, n_stations)),
            ]
            + cov_specs(start),
            out_specs=[
                pl.BlockSpec((6, tile_rows, GROUP, cells), lambda i: (0, 0, i, 0)),
                pl.BlockSpec((GROUP, n_stations), lambda i: (i, 0)),
            ],
            out_shape=[
                jax.ShapeDtypeStruct((6, tile_rows, size * GROUP, cells), bf16),
                jax.ShapeDtypeStruct((size * GROUP, n_stations), f32),
            ],
            scratch_shapes=[pltpu.VMEM((n, ext, GROUP, cells), f32) for n in (6, 6, 2, 2)]
            + [pltpu.VMEM((6 * groups * turned_size(tile_rows), 128), f32)],
            compiler_params=grant(22),
        )
        pf, s = window(where, lows[c], highs[c], wet, coef, station_row, *[flat] * groups)
        forecasts.append(shifted(pf, "cols"))
        sensed.append(shifted(s, "cols"))

    sensed_all = [sensed[c][d] for d in range(n_cols) for c in range(len(chunks))]
    gram = pl.pallas_call(
        functools.partial(gram_kernel, columns=columns),
        in_specs=[smem] + [pl.BlockSpec(memory_space=pltpu.VMEM)] * (2 + len(sensed_all)),
        out_specs=pl.BlockSpec(memory_space=pltpu.VMEM),
        out_shape=jax.ShapeDtypeStruct((columns + 8, total), f32),
        scratch_shapes=[
            pltpu.VMEM((total, n_stations), f32),
            pltpu.VMEM((columns + 8, n_stations), f32),
        ],
        name="gram",
        compiler_params=grant(2),
    )(where, weight_row, innovation, *sensed_all)
    gram_all = shifted(spread_sum(gram, "space"), "cols")
    mix = pl.pallas_call(
        functools.partial(factor_kernel, columns=columns),
        in_specs=[smem] + [pl.BlockSpec(memory_space=pltpu.VMEM)] * n_cols,
        out_specs=pl.BlockSpec(memory_space=pltpu.VMEM),
        out_shape=jax.ShapeDtypeStruct((columns + 16, total), bf16),
        scratch_shapes=[pltpu.VMEM((total, total), f32)],
        name="factor",
        compiler_params=grant(2),
    )(where, *gram_all)

    pieces = [forecasts[c][d] for d in range(n_cols) for c in range(len(chunks))]
    updated, mean_out = pl.pallas_call(
        functools.partial(mix_kernel, columns=columns),
        grid=(6,),
        in_specs=[
            smem,
            whole_spec((columns + 16, total)),
            pl.BlockSpec((1, tile_rows, cells), lambda f: (f, 0, 0)),
        ]
        + [
            pl.BlockSpec((1, tile_rows, p.shape[2], cells), lambda f: (f, 0, 0, 0)) for p in pieces
        ],
        out_specs=[
            pl.BlockSpec((columns, 1, tile_rows, cells), lambda f: (0, f, 0, 0)),
            pl.BlockSpec((1, tile_rows, piece), lambda f: (f, 0, 0)),
        ],
        out_shape=[
            jax.ShapeDtypeStruct((columns, 6, tile_rows, cells), f32),
            jax.ShapeDtypeStruct((6, tile_rows, piece), f32),
        ],
        scratch_shapes=[
            pltpu.VMEM((tile_rows, cells), f32),
            pltpu.VMEM((groups, columns * (tile_rows + 1) + 8, 128), f32),
        ],
        name="mix",
        compiler_params=grant(10),
    )(where, mix, mean_final, *pieces)
    return (mean_out, updated)


def solution(mesh):
    return jax.shard_map(
        local,
        mesh=mesh,
        in_specs=(
            P(None, "space", "cols"),
            P("cols", None, "space", None),
            P(),
            P("space"),
            P("space"),
            P("space"),
        ),
        out_specs=(P(None, "space", "cols"), P("cols", None, "space", None)),
        check_vma=False,
    )
```

```python
import functools

import jax
import jax.numpy as jnp
from jax import lax
from jax.experimental import pallas as pl
from jax.experimental.pallas import tpu as pltpu
from jax.sharding import PartitionSpec as P


ITERS = 4
DEPTH = 2 * ITERS
GROUP = 16

time_step = 0.5
gravity = 1.0
reduced_gravity = 0.125
coriolis = 0.3
friction = 0.05
layer_depths = (1.0, 2.0)

keep_part = 1.0 - time_step * friction
turn_part = time_step * coriolis
slope_part = 0.5 * time_step

f32 = jnp.float32
bf16 = jnp.bfloat16


def halo_rows():
    rows = []
    for layer in range(2):
        rows += [(3 * layer, d) for d in range(DEPTH - 1, 0, -1)]
    for layer in range(2):
        rows += [(3 * layer + 1, d) for d in range(DEPTH - 1, 0, -1)]
        rows += [(3 * layer + 2, d) for d in range(DEPTH - 2, 0, -1)]
    return rows


def turn(src_ref, src_row, stride, turned, base, tile_rows):
    pitch = GROUP + 1
    for k in range(GROUP):
        for r in range(0, tile_rows, 8):
            turned[pl.ds(base + r * pitch + k, 8, stride=pitch), :] = src_ref[
                pl.ds(k * stride + src_row + r, 8), :
            ]


def turned_row(turned, base, r):
    pitch = GROUP + 1
    return jnp.concatenate(
        [turned[pl.ds(base + r * pitch + 8 * kg, 8, stride=1), :] for kg in range(GROUP // 8)],
        axis=0,
    )


def turned_size(tile_rows):
    return tile_rows * (GROUP + 1) + 8


def pack_kernel(*refs, tile_rows, with_mean):
    cov_refs, (up_ref, down_ref, turned) = refs[:-3], refs[-3:]
    if with_mean:
        mean_ref, cov_refs = cov_refs[0], cov_refs[1:]
        piece = mean_ref.shape[2]
        for i in range(3):
            for ref, r in ((up_ref, tile_rows - DEPTH), (down_ref, 0)):
                value = jnp.concatenate(
                    [mean_ref[f, pl.ds(r, DEPTH), :] for f in (2 * i, 2 * i + 1)], axis=0
                )
                high = value.astype(bf16)
                low = (value - high.astype(f32)).astype(bf16)
                ref[len(halo_rows()) + i, :, pl.ds(0, piece)] = high
                ref[len(halo_rows()) + i, :, pl.ds(128, piece)] = low
    stride = 6 * tile_rows
    size = turned_size(tile_rows)
    groups = len(cov_refs)
    for f in range(6):
        for c in range(groups):
            turn(cov_refs[c], f * tile_rows, stride, turned, (f * groups + c) * size, tile_rows)

    def row(field, r):
        return jnp.concatenate(
            [turned_row(turned, (field * groups + c) * size, r) for c in range(groups)], axis=1
        )

    for i, (field, d) in enumerate(halo_rows()):
        for ref, r, side in ((up_ref, tile_rows - d, -1), (down_ref, d - 1, 1)):
            value = row(field, r)
            if d == DEPTH - 1 and field % 3 == 1:
                top = row(0, r + side)
                beyond = gravity * (top + row(3, r + side))
                if field > 3:
                    beyond = beyond - reduced_gravity * top
                value = value + (turn_part / keep_part) * row(field + 1, r)
                value = value - (side * slope_part / keep_part) * beyond
            ref[i] = value.astype(bf16)


def lane_steps(parts, lane):
    n = len(parts)
    right = [pltpu.roll(p, 1, 1) for p in parts]
    left = [pltpu.roll(p, 127, 1) for p in parts]
    out = []
    for i in range(n):
        before = jnp.where(lane == 0, right[i - 1] if i > 0 else 0.0, right[i])
        after = jnp.where(lane == 127, left[i + 1] if i < n - 1 else 0.0, left[i])
        out.append(after - before)
    return out


def station_hits(stations_ref, r, cells):
    position = lax.broadcasted_iota(jnp.int32, (cells, stations_ref.shape[1]), 0) + r * cells
    return position == stations_ref[...]


def mean_kernel(
    where_ref, mean_ref, mask_ref, stations_ref, observed_ref, weight_ref,
    wet_out, coef_out, final_out, innov_out, *, tile_rows, grid_rows,
):
    first_row = where_ref[0]
    ext, cells = mean_ref.shape[1:]
    wets = []
    for i in range(ext // 8):
        g = first_row - DEPTH + 8 * i
        inside = jnp.logical_and(g >= 0, g < grid_rows).astype(f32)
        start = pl.multiple_of(jnp.clip(g, 0, grid_rows - 8), 8)
        wets.append(mask_ref[pl.ds(start, 8), :].astype(f32) * inside)
    wet = jnp.concatenate(wets, axis=0)
    g_all = first_row - DEPTH + lax.broadcasted_iota(jnp.int32, (ext, cells), 0)
    keep = jnp.logical_and(g_all >= 0, g_all < grid_rows).astype(f32)
    lane_all = lax.broadcasted_iota(jnp.int32, (ext, cells), 1)

    def put(ref, index, value):
        rows = ref.shape[0] // (cells // 128)
        for c in range(cells // 128):
            ref[pl.ds(c * rows + index * ext, ext), :] = value[:, 128 * c : 128 * c + 128]

    put(wet_out, 0, wet * keep_part)
    put(wet_out, 1, wet * turn_part)
    put(wet_out, 2, wet * slope_part)

    def diff_rows(a):
        return 0.5 * (pltpu.roll(a, ext - 1, 0) - pltpu.roll(a, 1, 0))

    def diff_cols(a):
        after = jnp.where(lane_all == cells - 1, 0.0, pltpu.roll(a, cells - 1, 1))
        before = jnp.where(lane_all == 0, 0.0, pltpu.roll(a, 1, 1))
        return 0.5 * (after - before)

    state = [mean_ref[f] for f in range(6)]
    for t in range(ITERS):
        pressure_top = gravity * (state[0] + state[3])
        pressures = (pressure_top, pressure_top - reduced_gravity * state[0])
        fresh = []
        for layer in range(2):
            h, u, v = state[3 * layer : 3 * layer + 3]
            p = pressures[layer]
            u_new = wet * (u + time_step * (-diff_rows(p) + coriolis * v - friction * u))
            v_new = wet * (v + time_step * (-diff_cols(p) - coriolis * u - friction * v))
            depth = layer_depths[layer] + h
            h_new = h - time_step * (diff_rows(depth * u_new) + diff_cols(depth * v_new))
            for q, value in enumerate((depth, u_new, v_new)):
                put(coef_out, t * 6 + 3 * layer + q, slope_part * value)
            fresh += [h_new * keep, u_new, v_new]
        state = fresh
    for f in range(6):
        final_out[f] = state[f][DEPTH : DEPTH + tile_rows, :]
    surface = (state[0] + state[3])[DEPTH : DEPTH + tile_rows, :]
    n_stations = stations_ref.shape[1]
    sublane = lax.broadcasted_iota(jnp.int32, (8, n_stations), 0)
    picked = jnp.zeros((8, n_stations), f32)
    for r in range(tile_rows):
        hits = station_hits(stations_ref, r, cells).astype(f32)
        block = surface[r // 8 * 8 : r // 8 * 8 + 8, :]
        values = jnp.dot(block, hits, precision=lax.Precision.HIGHEST, preferred_element_type=f32)
        picked = picked + jnp.where(sublane == r % 8, values, 0.0)
    at_station = jnp.sum(picked, axis=0, keepdims=True)
    innovation = weight_ref[...] * (observed_ref[...] - at_station)
    innov_out[...] = jnp.where(sublane == 0, innovation, 0.0)


def window_kernel(
    where_ref, low_ref, high_ref, wet_ref, coef_ref, stations_ref, *refs,
    tile_rows, grid_rows,
):
    cov_refs, (pf_out, sensed_out, state_a, state_b, press, flux, turned) = refs[:-7], refs[-7:]
    first_row = where_ref[0]
    ext = tile_rows + 2 * DEPTH
    groups = len(cov_refs)
    cells = 128 * groups
    stride = 6 * tile_rows
    halves = range(GROUP // 8)

    def at(ref, field, r, kg):
        return [ref[field, r, pl.ds(8 * kg, 8), pl.ds(128 * c, 128)] for c in range(groups)]

    def put(ref, field, r, kg, parts):
        for c in range(groups):
            ref[field, r, pl.ds(8 * kg, 8), pl.ds(128 * c, 128)] = parts[c]

    def spread(ref, index, r):
        rows = ref.shape[0] // groups
        return [ref[pl.ds(c * rows + index * ext + r, 8, stride=0), :] for c in range(groups)]

    size = turned_size(tile_rows)
    for f in range(6):
        for c in range(groups):
            base = (f * groups + c) * size
            turn(cov_refs[c], f * tile_rows, stride, turned, base, tile_rows)
            for r in range(tile_rows):
                state_a[f, DEPTH + r, :, pl.ds(128 * c, 128)] = turned_row(turned, base, r)
    for i, (field, d) in enumerate(halo_rows()):
        state_a[field, DEPTH - d] = low_ref[i].astype(f32)
        state_a[field, DEPTH + tile_rows + d - 1] = high_ref[i].astype(f32)
    for layer in range(2):
        for r in (1, ext - 2):
            state_a[3 * layer + 2, r] = jnp.zeros((GROUP, cells), f32)
        for r in (0, ext - 1):
            state_a[3 * layer, r] = jnp.zeros((GROUP, cells), f32)

    def press_of(top, bottom):
        p_top = gravity * (top + bottom)
        return p_top, p_top - reduced_gravity * top

    def first_press(r, carry):
        press[0, r], press[1, r] = press_of(state_a[0, r], state_a[3, r])
        return carry

    lax.fori_loop(0, ext, first_press, 0, unroll=2)
    lane = lax.broadcasted_iota(jnp.int32, (8, 128), 1)

    def move(t, src, dst, r_first, count, edge=False):
        stores = []
        for r in [r_first + k for k in range(count)]:
            wet_a, wet_b, wet_c = (spread(wet_ref, q, r) for q in range(3))
            for layer in range(2):
                depth, mu, mv = (spread(coef_ref, t * 6 + 3 * layer + q, r) for q in range(3))
                for kg in halves:
                    h = at(src, 3 * layer, r, kg)
                    u = at(src, 3 * layer + 1, r, kg)
                    v = at(src, 3 * layer + 2, r, kg)
                    before = at(press, layer, r - 1, kg)
                    after = at(press, layer, r + 1, kg)
                    if edge:
                        u_new, along = [], []
                        for c in range(groups):
                            u_c = (
                                wet_a[c] * u[c] + wet_b[c] * v[c] - wet_c[c] * (after[c] - before[c])
                            )
                            along.append(depth[c] * u_c + h[c] * mu[c])
                        stores.append((flux, layer, r, kg, along))
                        continue
                    slope = lane_steps(at(press, layer, r, kg), lane)
                    u_new, v_new, along, cross = [], [], [], []
                    for c in range(groups):
                        u_c = wet_a[c] * u[c] + wet_b[c] * v[c] - wet_c[c] * (after[c] - before[c])
                        v_c = wet_a[c] * v[c] - wet_b[c] * u[c] - wet_c[c] * slope[c]
                        u_new.append(u_c)
                        v_new.append(v_c)
                        along.append(depth[c] * u_c + h[c] * mu[c])
                        cross.append(depth[c] * v_c + h[c] * mv[c])
                    cross = lane_steps(cross, lane)
                    part = [h[c] - cross[c] for c in range(groups)]
                    stores += [
                        (dst, 3 * layer, r, kg, part),
                        (dst, 3 * layer + 1, r, kg, u_new),
                        (dst, 3 * layer + 2, r, kg, v_new),
                        (flux, layer, r, kg, along),
                    ]
        for store in stores:
            put(*store)

    def rise(t, dst, r_first, count):
        stores = []
        for r in [r_first + k for k in range(count)]:
            g = first_row - DEPTH + r
            keep = jnp.where(jnp.logical_and(g >= 0, g < grid_rows), 1.0, 0.0).astype(f32)
            for kg in halves:
                fresh = []
                for layer in range(2):
                    part = at(dst, 3 * layer, r, kg)
                    before, after = at(flux, layer, r - 1, kg), at(flux, layer, r + 1, kg)
                    fresh.append(
                        [keep * (part[c] - (after[c] - before[c])) for c in range(groups)]
                    )
                    stores.append((dst, 3 * layer, r, kg, fresh[-1]))
                if t < ITERS - 1:
                    both = [press_of(fresh[0][c], fresh[1][c]) for c in range(groups)]
                    for layer in range(2):
                        stores.append((press, layer, r, kg, [p[layer] for p in both]))
        for store in stores:
            put(*store)

    src, dst = state_a, state_b
    for t in range(ITERS):
        first = 2 * t + 2
        rows = ext - 4 * t - 4
        pace = 4 if rows % 4 == 0 else (2 if rows % 2 == 0 else 1)
        move(t, src, dst, first - 1, 1, edge=True)
        move(t, src, dst, first + rows, 1, edge=True)

        def move_body(i, carry, t=t, src=src, dst=dst, first=first, pace=pace):
            move(t, src, dst, first + pace * i, pace)
            return carry

        lax.fori_loop(0, rows // pace, move_body, 0)

        def rise_body(i, carry, t=t, dst=dst, first=first, pace=pace):
            rise(t, dst, first + pace * i, pace)
            return carry

        lax.fori_loop(0, rows // pace, rise_body, 0)
        src, dst = dst, src

    n_stations = stations_ref.shape[1]
    total = jnp.zeros((3 * GROUP, n_stations), f32)
    for r in range(tile_rows):
        for f in range(6):
            pf_out[f, r] = src[f, DEPTH + r].astype(bf16)
        surface = src[0, DEPTH + r] + src[3, DEPTH + r]
        high = surface.astype(bf16)
        rest = surface - high.astype(f32)
        middle = rest.astype(bf16)
        low = (rest - middle.astype(f32)).astype(bf16)
        pieces = jnp.concatenate([high, middle, low], axis=0)
        hits = station_hits(stations_ref, r, cells).astype(f32).astype(bf16)
        total = total + jnp.dot(pieces, hits, preferred_element_type=f32)
    sensed_out[...] = (
        total[:GROUP] + (total[GROUP : 2 * GROUP] + total[2 * GROUP : 3 * GROUP])
    )


def gram_kernel(where_ref, weight_ref, innov_ref, *refs, columns):
    sensed_refs, out_ref, both, left = refs[:-3], refs[-3], refs[-2], refs[-1]
    index = where_ref[1]
    count = both.shape[0] // columns
    each = len(sensed_refs) // count
    for d in range(count):
        start = pl.multiple_of(lax.rem(index + d, count) * columns, 8)
        for ref in sensed_refs[d * each : (d + 1) * each]:
            size = ref.shape[0]
            both[pl.ds(start, size), :] = ref[...] * weight_ref[...]
            start = pl.multiple_of(start + size, 8)
    left[pl.ds(0, columns), :] = both[pl.ds(pl.multiple_of(index * columns, 8), columns), :]
    left[pl.ds(columns, 8), :] = innov_ref[...]
    out_ref[...] = lax.dot_general(
        left[...],
        both[...],
        (((1,), (1,)), ((), ())),
        precision=lax.Precision.HIGHEST,
        preferred_element_type=f32,
    )


def factor_kernel(where_ref, *refs, columns):
    gram_refs, mix_out, scr = refs[:-2], refs[-2], refs[-1]
    index = where_ref[1]
    count = len(gram_refs)
    total = count * columns
    for d in range(count):
        start = pl.multiple_of(lax.rem(index + d, count) * columns, 8)
        scr[pl.ds(start, columns), :] = gram_refs[d][pl.ds(0, columns), :]
    blocks = total // 8
    lane = lax.broadcasted_iota(jnp.int32, (8, total), 1)
    sub = lax.broadcasted_iota(jnp.int32, (8, total), 0)
    eye = [(lane == sub + 8 * b).astype(f32) for b in range(blocks)]
    m = [scr[pl.ds(8 * b, 8), :] + eye[b] for b in range(blocks)]
    w = list(eye)

    def column(x, j):
        return jnp.broadcast_to(x[:, j : j + 1], (8, total))

    def row(x, i):
        return jnp.broadcast_to(x[i : i + 1, :], (8, total))

    scaled = []
    for b in range(blocks):
        heads = [column(m[b], 8 * b + i) for i in range(8)]
        z_m, z_w, low = m[b], w[b], w[b]
        pivots = jnp.ones((8, total), f32)
        for i in range(8):
            pivot = row(heads[i], i)
            pivots = jnp.where(sub == i, pivot, pivots)
            inverse = 1.0 / pivot
            here = sub == i
            head = heads[i]
            for k in range(i + 1, 8):
                factor = row(heads[k], i) * inverse
                heads[k] = jnp.where(here, factor, heads[k] - head * factor)
            row_m = row(z_m, i) * inverse
            row_w = row(z_w, i) * inverse
            z_m = jnp.where(here, row_m, z_m - head * row_m)
            z_w = jnp.where(here, row_w, z_w - head * row_w)
            low = jnp.where(sub > i, low - head * row_w, low)
        scaled.append(low / jnp.sqrt(pivots))
        rows_m = [row(z_m, i) for i in range(8)]
        rows_w = [row(z_w, i) for i in range(8)]
        for q in range(b + 1, blocks):
            tails = [column(m[q], 8 * b + i) for i in range(8)]
            m[q] = m[q] - tree_sum([tails[i] * rows_m[i] for i in range(8)])
            w[q] = w[q] - tree_sum([tails[i] * rows_w[i] for i in range(8)])
    target = gram_refs[0][pl.ds(columns, 1), :]
    weights = jnp.zeros((8, total), f32)
    for b in range(blocks):
        scr[pl.ds(8 * b, 8), :] = scaled[b]
        half = jnp.sum(scaled[b] * target, axis=1, keepdims=True)
        weights = weights + scaled[b] * half
    weights = jnp.sum(weights, axis=0, keepdims=True)
    shift = lax.rem(total - index * columns, total)
    mine = scr[pl.ds(pl.multiple_of(index * columns, 8), columns), :]
    mix_out[pl.ds(0, columns), :] = pltpu.roll(mine, shift, 1).astype(bf16)
    weights = pltpu.roll(jnp.broadcast_to(weights, (8, total)), shift, 1)
    high = weights.astype(bf16)
    low = (weights - high.astype(f32)).astype(bf16)
    pad = jnp.zeros((8, total), f32)
    rows = jnp.where(sub == 0, high.astype(f32), jnp.where(sub == 1, low.astype(f32), 0.0))
    mix_out[pl.ds(columns, 16), :] = jnp.concatenate([rows, pad], axis=0).astype(bf16)


def tree_sum(values):
    while len(values) > 1:
        values = [values[i] + values[i + 1] for i in range(0, len(values), 2)]
    return values[0]


def mix_kernel(where_ref, mix_ref, mean_ref, *refs, columns):
    piece_refs, (cov_out, mean_out, scr, turned) = refs[:-4], refs[-4:]
    tile_rows, cells = mean_ref.shape[1:]
    groups = cells // 128
    piece = mean_out.shape[2]
    mix = mix_ref[...]
    pitch = tile_rows + 1
    for r in range(tile_rows):
        stack = jnp.concatenate([ref[0, r] for ref in piece_refs], axis=0)
        result = jnp.dot(mix, stack, preferred_element_type=f32)
        for c in range(groups):
            for j in range(0, columns, 8):
                turned[c, pl.ds(j * pitch + r, 8, stride=pitch), :] = result[
                    j : j + 8, 128 * c : 128 * c + 128
                ]
        scr[pl.ds(r, 1), :] = result[columns : columns + 1] + result[columns + 1 : columns + 2]
    for j in range(columns):
        for c in range(groups):
            for r in range(0, tile_rows, 8):
                cov_out[j, 0, pl.ds(r, 8), pl.ds(128 * c, 128)] = turned[
                    c, pl.ds(j * pitch + r, 8, stride=1), :
                ]
    whole = mean_ref[0] + scr[...]
    shift = lax.rem(cells - where_ref[1] * piece, cells)
    mean_out[0] = pltpu.roll(whole, shift, 1)[:, :piece]


def spread_sum(value, axis):
    count = lax.axis_size(axis)
    if count & (count - 1):
        return lax.psum(value, axis)
    step = 1
    while step < count:
        value = value + lax.ppermute(value, axis, [(i, i ^ step) for i in range(count)])
        step *= 2
    return value


def shifted(value, axis):
    count = lax.axis_size(axis)
    return [value] + [
        lax.ppermute(value, axis, [((i + d) % count, i) for i in range(count)])
        for d in range(1, count)
    ]


def grant(mib):
    return pltpu.CompilerParams(vmem_limit_bytes=mib << 20)


def in_hbm(value):
    return pltpu.with_memory_space_constraint(value, pltpu.HBM)


def whole_spec(shape):
    return pl.BlockSpec(shape, lambda *_: (0,) * len(shape))


def chunk_list(count):
    if count < 3:
        return [(g, 1) for g in range(count)]
    return [(0, 1), (1, count - 2), (count - 1, 1)]


def local(mean_state, covariance, land_mask, stations, observed, obs_weight):
    columns, _, tile_rows, cells = covariance.shape
    piece = mean_state.shape[2]
    n_space = lax.axis_size("space")
    n_cols = lax.axis_size("cols")
    total = columns * n_cols
    grid_rows = tile_rows * n_space
    ext = tile_rows + 2 * DEPTH
    n_stations = stations.shape[0]
    chunks = chunk_list(columns // GROUP)
    n_halo = len(halo_rows())
    groups = cells // 128
    space_index = lax.axis_index("space")
    column_index = lax.axis_index("cols")
    first_row = space_index * tile_rows
    where = jnp.stack([first_row, column_index]).astype(jnp.int32)
    up = [(i, i + 1) for i in range(n_space - 1)]
    down = [(i + 1, i) for i in range(n_space - 1)]
    smem = pl.BlockSpec(memory_space=pltpu.SMEM)

    flat = covariance.reshape(columns * 6 * tile_rows, cells)
    span = GROUP * 6 * tile_rows


    def cov_specs(start):
        return [pl.BlockSpec((span, 128), lambda i, g=g: (start + i, g)) for g in range(groups)]

    halo_spec = pl.BlockSpec((n_halo, GROUP, cells), lambda i: (0, i, 0))
    lows, highs = [], []
    source = flat
    for c, (start, size) in enumerate(chunks):
        rows = n_halo + 3 if c == 0 else n_halo
        halo_shape = jax.ShapeDtypeStruct((rows, size * GROUP, cells), bf16)
        halo_out = pl.BlockSpec((rows, GROUP, cells), lambda i: (0, i, 0))
        going_up, going_down = pl.pallas_call(
            functools.partial(pack_kernel, tile_rows=tile_rows, with_mean=c == 0),
            grid=(size,),
            in_specs=[whole_spec(mean_state.shape)] * (c == 0) + cov_specs(start),
            out_specs=[halo_out] * 2,
            out_shape=[halo_shape, halo_shape],
            scratch_shapes=[pltpu.VMEM((6 * groups * turned_size(tile_rows), 128), f32)],
            compiler_params=grant(9),
        )(*[in_hbm(mean_state)] * (c == 0), *[in_hbm(source)] * groups)
        source, going_up, going_down = lax.optimization_barrier((flat, going_up, going_down))
        lows.append(lax.ppermute(going_up, "space", up))
        highs.append(lax.ppermute(going_down, "space", down))


    parts = jnp.concatenate([lows[0][n_halo:], highs[0][n_halo:]], axis=0)
    parts = lax.optimization_barrier(parts).astype(f32)
    halo = (parts[:, :, :piece] + parts[:, :, 128 : 128 + piece]).reshape(12, DEPTH, piece)
    mean_ext = jnp.concatenate([halo[:6], mean_state, halo[6:]], axis=1)
    mean_ext = lax.all_gather(mean_ext, "cols", axis=2, tiled=True)
    station_row = (stations - first_row * cells).astype(jnp.int32)[None, :]
    weight_row = obs_weight[None, :]
    mean_run = pl.pallas_call(
        functools.partial(mean_kernel, tile_rows=tile_rows, grid_rows=grid_rows),
        in_specs=[smem] + [pl.BlockSpec(memory_space=pltpu.VMEM)] * 5,
        out_specs=[pl.BlockSpec(memory_space=pltpu.VMEM)] * 4,
        out_shape=[
            jax.ShapeDtypeStruct((groups * 3 * ext, 128), f32),
            jax.ShapeDtypeStruct((groups * ITERS * 6 * ext, 128), f32),
            jax.ShapeDtypeStruct((6, tile_rows, cells), f32),
            jax.ShapeDtypeStruct((8, n_stations), f32),
        ],
        name="mean_window",
        compiler_params=grant(4),
    )
    wet, coef, mean_final, innovation = mean_run(
        where, mean_ext, land_mask, station_row, observed[None, :], weight_row
    )

    forecasts, sensed = [], []
    for c, (start, size) in enumerate(chunks):
        window = pl.pallas_call(
            functools.partial(window_kernel, tile_rows=tile_rows, grid_rows=grid_rows),
            grid=(size,),
            in_specs=[
                smem,
                halo_spec,
                halo_spec,
                whole_spec((groups * 3 * ext, 128)),
                whole_spec((groups * ITERS * 6 * ext, 128)),
                whole_spec((1, n_stations)),
            ]
            + cov_specs(start),
            out_specs=[
                pl.BlockSpec((6, tile_rows, GROUP, cells), lambda i: (0, 0, i, 0)),
                pl.BlockSpec((GROUP, n_stations), lambda i: (i, 0)),
            ],
            out_shape=[
                jax.ShapeDtypeStruct((6, tile_rows, size * GROUP, cells), bf16),
                jax.ShapeDtypeStruct((size * GROUP, n_stations), f32),
            ],
            scratch_shapes=[pltpu.VMEM((n, ext, GROUP, cells), f32) for n in (6, 6, 2, 2)]
            + [pltpu.VMEM((6 * groups * turned_size(tile_rows), 128), f32)],
            compiler_params=grant(22),
        )
        pf, s = window(where, lows[c], highs[c], wet, coef, station_row, *[flat] * groups)
        forecasts.append(shifted(pf, "cols"))
        sensed.append(shifted(s, "cols"))

    sensed_all = [sensed[c][d] for d in range(n_cols) for c in range(len(chunks))]
    gram = pl.pallas_call(
        functools.partial(gram_kernel, columns=columns),
        in_specs=[smem] + [pl.BlockSpec(memory_space=pltpu.VMEM)] * (2 + len(sensed_all)),
        out_specs=pl.BlockSpec(memory_space=pltpu.VMEM),
        out_shape=jax.ShapeDtypeStruct((columns + 8, total), f32),
        scratch_shapes=[
            pltpu.VMEM((total, n_stations), f32),
            pltpu.VMEM((columns + 8, n_stations), f32),
        ],
        name="gram",
        compiler_params=grant(2),
    )(where, weight_row, innovation, *sensed_all)
    gram_all = shifted(spread_sum(gram, "space"), "cols")
    mix = pl.pallas_call(
        functools.partial(factor_kernel, columns=columns),
        in_specs=[smem] + [pl.BlockSpec(memory_space=pltpu.VMEM)] * n_cols,
        out_specs=pl.BlockSpec(memory_space=pltpu.VMEM),
        out_shape=jax.ShapeDtypeStruct((columns + 16, total), bf16),
        scratch_shapes=[pltpu.VMEM((total, total), f32)],
        name="factor",
        compiler_params=grant(2),
    )(where, *gram_all)

    pieces = [forecasts[c][d] for d in range(n_cols) for c in range(len(chunks))]
    updated, mean_out = pl.pallas_call(
        functools.partial(mix_kernel, columns=columns),
        grid=(6,),
        in_specs=[
            smem,
            whole_spec((columns + 16, total)),
            pl.BlockSpec((1, tile_rows, cells), lambda f: (f, 0, 0)),
        ]
        + [
            pl.BlockSpec((1, tile_rows, p.shape[2], cells), lambda f: (f, 0, 0, 0)) for p in pieces
        ],
        out_specs=[
            pl.BlockSpec((columns, 1, tile_rows, cells), lambda f: (0, f, 0, 0)),
            pl.BlockSpec((1, tile_rows, piece), lambda f: (f, 0, 0)),
        ],
        out_shape=[
            jax.ShapeDtypeStruct((columns, 6, tile_rows, cells), f32),
            jax.ShapeDtypeStruct((6, tile_rows, piece), f32),
        ],
        scratch_shapes=[
            pltpu.VMEM((tile_rows, cells), f32),
            pltpu.VMEM((groups, columns * (tile_rows + 1) + 8, 128), f32),
        ],
        name="mix",
        compiler_params=grant(10),
    )(where, mix, mean_final, *pieces)
    return (mean_out, updated)


def solution(mesh):
    return jax.shard_map(
        local,
        mesh=mesh,
        in_specs=(
            P(None, "space", "cols"),
            P("cols", None, "space", None),
            P(),
            P("space"),
            P("space"),
            P("space"),
        ),
        out_specs=(P(None, "space", "cols"), P("cols", None, "space", None)),
        check_vma=False,
    )
```
